32 devices in a mesh: dp: 8 (over z, x), seq: 4 (over y, core).
Axes of the slice: x: 2, y: 2, z: 4, core: 2. Of those that a mesh axis runs over, the one named last changes fastest.
Arguments:
- queries: bfloat16 [8, 512, 2048], P('dp', 'seq'), may hold values from -72 to 72
- hit_keys: bfloat16 [8, 512, 2048], P('dp', 'seq'), may hold values from -12 to 12
- hit_values: bfloat16 [8, 512, 2048], P('dp', 'seq'), may hold values from -6 to 6
- hit_counts: int32 [8], P('dp'), may hold values from 128 to 512, as said below
- master_weight: float32 [8, 256, 2048], P('dp', None, 'seq'), may hold values from -0.5 to 0.5
- first_moment: float32 [8, 256, 2048], P('dp', None, 'seq'), may hold values from -4 to 4
- second_moment: float32 [8, 256, 2048], P('dp', None, 'seq'), may hold values from 0.1 to 4
- gradient: float32 [8, 256, 2048], P('dp', None, 'seq'), may hold values from -6 to 6
- owner_bucket: int32 [8], replicated, may hold values from 0 to 7, each once
Outputs:
- projected: bfloat16 [8, 512, 2048], P('dp', 'seq')
- new_master: float32 [8, 256, 2048], P('dp', None, 'seq')
- new_first: float32 [8, 256, 2048], P('dp', None, 'seq')
- new_second: float32 [8, 256, 2048], P('dp', None, 'seq')
The draws below stay inside these ranges and needn't reach their ends.
Inputs may be any that keep to these rules, and one draw needn't show every extreme that they name: The valid hits of event e are its first hit_counts[e] slots; some event is full. `owner_bucket`: each bucket is held by exactly one owner.
All inputs are finite; a program needn't handle non-finite values.
Results may differ from the reference program's by a relative error of at most 0.0063.
Values may be sent and summed in bfloat16 or wider, within the bound.
No kernel may reach another device: no remote copies, remote signals or barrier semaphores. Data moves between devices by JAX's collectives and lax.ppermute only.
A program may use at most 64 MiB of HBM per device.

```python
import math
import jax
import jax.numpy as jnp
from jax import lax

HEAD_DIM = 128
D = 2048
SEQ_LEN = 512
BROWS = 256
N_DP = 8


def drawn(key):
    query_key = jax.random.fold_in(key, 11)
    keys_key = jax.random.fold_in(key, 12)
    shape = (N_DP, SEQ_LEN, D)
    query = jnp.clip(2.0 * jax.random.normal(query_key, shape, jnp.float32), -12.0, 12.0)
    keyarr = jnp.clip(2.0 * jax.random.normal(keys_key, shape, jnp.float32), -12.0, 12.0)
    return (query, keyarr)


def draw_queries(key, part):
    return drawn(key)[0].astype(jnp.bfloat16)


def draw_hit_keys(key, part):
    return drawn(key)[1].astype(jnp.bfloat16)


def draw_hit_counts(key, part):
    base = jax.random.randint(jax.random.fold_in(key, 21), (N_DP,), SEQ_LEN // 4, SEQ_LEN + 1, jnp.int32)
    spot = jax.random.randint(jax.random.fold_in(key, 22), (), 0, N_DP, jnp.int32)
    return jnp.where(jnp.arange(N_DP, dtype=jnp.int32) == spot, SEQ_LEN, base).astype(jnp.int32)


def levels(stream_key, dims, shards, least, largest):
    gain, own = 1.0, jax.random.fold_in(stream_key, 6)
    for dim, parts in shards:
        heights = jnp.exp(jax.random.uniform(jax.random.fold_in(own, dim), (parts,), jnp.float32, least / len(shards), largest / len(shards)))
        gain = gain * jnp.repeat(heights, dims[dim] // parts).reshape([-1 if axis == dim else 1 for axis in range(len(dims))])
    return gain


def bell_draw(rng, shape, scale, reach, split=(), kind=jnp.bfloat16):
    drawn = scale * jax.random.normal(rng, shape, jnp.float32)
    if split:
        drawn = drawn * levels(rng, shape, split, -0.22, 0.18)
    return jnp.clip(drawn, -reach, reach).astype(kind)


def setup_inputs(seed: int = 0) -> dict:
    streams_of = jax.random.split(jax.random.key(seed), 10)
    queries = draw_queries(jax.random.fold_in(streams_of[9], 71), 0)
    hit_keys = draw_hit_keys(jax.random.fold_in(streams_of[9], 71), 0)
    hit_values = bell_draw(streams_of[2], (N_DP, SEQ_LEN, D), 1.0, 6.0, ((0, 8), (1, 4)))
    hit_counts = draw_hit_counts(jax.random.fold_in(streams_of[9], 71), 0)
    master_weight = bell_draw(streams_of[4], (N_DP, BROWS, D), (D // 16) ** -0.5, 0.5, ((0, 8), (2, 4)), jnp.float32)
    first_moment = bell_draw(streams_of[5], (N_DP, BROWS, D), 0.5, 4.0, ((0, 8), (2, 4)), jnp.float32)
    second_moment = jnp.clip(jnp.exp(math.log(4.0) - 3.6888794 * jax.random.uniform(streams_of[6], (N_DP, BROWS, D), jnp.float32) ** levels(streams_of[6], (N_DP, BROWS, D), ((0, 8), (2, 4)), -0.2, 0.2)), 0.1, 4.0)
    gradient = bell_draw(streams_of[7], (N_DP, BROWS, D), 1.0, 6.0, ((0, 8), (2, 4)), jnp.float32)
    owner_bucket = jax.random.permutation(streams_of[8], N_DP).astype(jnp.int32)
    return {"queries": queries, "hit_keys": hit_keys, "hit_values": hit_values, "hit_counts": hit_counts, "master_weight": master_weight, "first_moment": first_moment, "second_moment": second_moment, "gradient": gradient, "owner_bucket": owner_bucket}


beta_one = 0.9
beta_two = 0.999
learn_rate = 0.003
weight_decay = 0.1
epsilon = 1e-08
step_count = 10.0
block_rows = 512
wider_rows = 768

def adam_update(master_weight, first_moment, second_moment, gradient):
    new_first = beta_one * first_moment + (1.0 - beta_one) * gradient
    new_second = beta_two * second_moment + (1.0 - beta_two) * gradient * gradient
    first_hat = new_first / (1.0 - beta_one ** step_count)
    second_hat = new_second / (1.0 - beta_two ** step_count)
    new_master = master_weight - learn_rate * (first_hat / (jnp.sqrt(second_hat) + epsilon) + weight_decay * master_weight)
    return (new_master, new_first, new_second)

def attend_head(head_query, head_keys, head_values, count):
    length = head_query.shape[0]
    block = wider_rows if length % wider_rows == 0 else min(block_rows, length)
    scale = head_query.shape[1] ** (-0.5)
    valid = lax.broadcasted_iota(jnp.int32, (1, length), 1) < count

    def one_block(rows):
        scores = lax.dot_general(rows, head_keys, (((1,), (1,)), ((), ())), preferred_element_type=jnp.float32) * scale
        scores = jnp.where(valid, scores, -jnp.inf)
        top = lax.optimization_barrier(jnp.max(scores, axis=1, keepdims=True))
        expo = jnp.exp(scores - top)
        weights = (expo / lax.optimization_barrier(jnp.sum(expo, axis=1, keepdims=True))).astype(jnp.bfloat16)
        return jnp.dot(weights, head_values, preferred_element_type=jnp.float32).astype(jnp.bfloat16)
    blocks = head_query.reshape(length // block, block, head_query.shape[1])
    return lax.map(one_block, blocks).reshape(length, head_query.shape[1])

def reference(queries, hit_keys, hit_values, hit_counts, master_weight, first_moment, second_moment, gradient, owner_bucket):
    new_master, new_first, new_second = adam_update(master_weight, first_moment, second_moment, gradient)
    weight_half = new_master.astype(jnp.bfloat16)
    placed = jnp.zeros_like(weight_half).at[owner_bucket].set(weight_half)
    projection = placed.reshape(D, D)
    head_count = D // HEAD_DIM

    def one_event(inputs):
        event_query, event_keys, event_values, count = inputs

        def one_head(index):
            start = (index * HEAD_DIM).astype(jnp.int32)
            head_query = lax.dynamic_slice_in_dim(event_query, start, HEAD_DIM, 1)
            head_keys = lax.dynamic_slice_in_dim(event_keys, start, HEAD_DIM, 1)
            head_values = lax.dynamic_slice_in_dim(event_values, start, HEAD_DIM, 1)
            return attend_head(head_query, head_keys, head_values, count)
        outputs = lax.map(one_head, jnp.arange(head_count, dtype=jnp.int32))
        joined = jnp.moveaxis(outputs, 0, 1).reshape(SEQ_LEN, D)
        return jnp.dot(joined, projection, preferred_element_type=jnp.float32).astype(jnp.bfloat16)
    projected = lax.map(one_event, (queries, hit_keys, hit_values, hit_counts))
    return (projected, new_master, new_first, new_second)
```

```python
import functools
import math

import jax
import jax.numpy as jnp
from jax import lax
from jax.experimental import pallas as pl
from jax.experimental.pallas import tpu as pltpu
from jax.sharding import PartitionSpec as P

HEAD_DIM = 128

beta_one = 0.9
beta_two = 0.999
learn_rate = 0.003
weight_decay = 0.1
epsilon = 1e-08
step_count = 10.0


def adam_update(master_weight, first_moment, second_moment, gradient):
    new_first = beta_one * first_moment + (1.0 - beta_one) * gradient
    new_second = beta_two * second_moment + (1.0 - beta_two) * gradient * gradient
    first_hat = new_first / (1.0 - beta_one**step_count)
    second_hat = new_second / (1.0 - beta_two**step_count)
    new_master = master_weight - learn_rate * (
        first_hat / (jnp.sqrt(second_hat) + epsilon) + weight_decay * master_weight
    )
    return (new_master, new_first, new_second)


def attend_kernel(n_keys, info_ref, *refs):
    query_refs, pair_refs = refs[:2], refs[2 : 2 + n_keys]
    out_ref, keys, values = refs[2 + n_keys :]
    rows, wide = query_refs[0].shape
    count = info_ref[0]
    columns = []
    for i, ref in enumerate(pair_refs):
        keys[i * rows : (i + 1) * rows, :] = ref[0]
        values[i * rows : (i + 1) * rows, :] = ref[1]
        base = info_ref[1 + i] * rows
        columns.append(base + lax.broadcasted_iota(jnp.int32, (1, rows), 1))
    valid = jnp.concatenate(columns, axis=1) < count
    factor = HEAD_DIM ** (-0.5) * math.log2(math.e)
    for block, query_ref in enumerate(query_refs):
        for head in range(wide // HEAD_DIM):
            lanes = slice(head * HEAD_DIM, (head + 1) * HEAD_DIM)
            scores = lax.dot_general(
                query_ref[:, lanes],
                keys[:, lanes],
                (((1,), (1,)), ((), ())),
                preferred_element_type=jnp.float32,
            )
            scores = jnp.where(valid, scores, -1e30)
            top = jnp.max(scores, axis=1, keepdims=True)
            expo = jnp.exp2((scores - top) * factor)
            total = jnp.sum(expo, axis=1, keepdims=True)
            weights = (expo * (1.0 / total)).astype(jnp.bfloat16)
            out_ref[block, :, lanes] = jnp.dot(
                weights, values[:, lanes], preferred_element_type=jnp.float32
            ).astype(jnp.bfloat16)


def attend(info, query_blocks, pairs):
    rows, wide = query_blocks[0].shape
    n_keys = len(pairs)
    work = 4 * 2 * rows * n_keys * rows * wide
    moved = 2 * (4 * rows * wide + 2 * n_keys * rows * wide)
    return pl.pallas_call(
        functools.partial(attend_kernel, n_keys),
        out_shape=jax.ShapeDtypeStruct((2, rows, wide), jnp.bfloat16),
        in_specs=[pl.BlockSpec(memory_space=pltpu.SMEM)]
        + [pl.BlockSpec(memory_space=pltpu.VMEM)] * (2 + n_keys),
        out_specs=pl.BlockSpec(memory_space=pltpu.VMEM),
        scratch_shapes=[pltpu.VMEM((n_keys * rows, wide), jnp.bfloat16)] * 2,
        cost_estimate=pl.CostEstimate(flops=work, bytes_accessed=moved, transcendentals=0),
        name="attend",
    )(info, *query_blocks, *pairs)


def project_kernel(n_att, n_weights, info_ref, *refs):
    att_refs, weight_refs = refs[:n_att], refs[n_att : n_att + n_weights]
    out_ref, held = refs[n_att + n_weights :]
    _, rows, wide = att_refs[0].shape
    depth = weight_refs[0].shape[0]
    parts = wide // depth
    for slot, ref in enumerate(att_refs):
        flip = slot % 2
        for block in range(2):
            for part in range(parts):
                held[slot * parts + part, block * rows : (block + 1) * rows, :] = ref[
                    block ^ flip, :, part * depth : (part + 1) * depth
                ]
    total = None
    for i, ref in enumerate(weight_refs):
        term = jnp.dot(held[info_ref[i]], ref[...], preferred_element_type=jnp.float32)
        total = term if total is None else total + term
    total = total.astype(jnp.bfloat16)
    out_ref[0] = total[:rows]
    out_ref[1] = total[rows:]


def project(info, att, weights):
    _, rows, wide = att[0].shape
    depth, columns = weights[0].shape
    work = 2 * 2 * rows * len(att) * wide * columns
    moved = 2 * (2 * rows * len(att) * wide + len(weights) * depth * columns)
    return pl.pallas_call(
        functools.partial(project_kernel, len(att), len(weights)),
        out_shape=jax.ShapeDtypeStruct((2, rows, columns), jnp.bfloat16),
        in_specs=[pl.BlockSpec(memory_space=pltpu.SMEM)]
        + [pl.BlockSpec(memory_space=pltpu.VMEM)] * (len(att) + len(weights)),
        out_specs=pl.BlockSpec(memory_space=pltpu.VMEM),
        scratch_shapes=[pltpu.VMEM((len(att) * wide // depth, 2 * rows, depth), jnp.bfloat16)],
        cost_estimate=pl.CostEstimate(flops=work, bytes_accessed=moved, transcendentals=0),
        name="project",
    )(info, *att, *weights)


def place_kernel(n, info_ref, *refs):
    out_ref = refs[n]
    columns = refs[0].shape[1]
    for i in range(n):
        start = pl.multiple_of(info_ref[i] * columns, columns)
        out_ref[:, pl.ds(start, columns)] = refs[i][...]


def place(info, blocks):
    rows, columns = blocks[0].shape
    return pl.pallas_call(
        functools.partial(place_kernel, len(blocks)),
        out_shape=jax.ShapeDtypeStruct((rows, columns * len(blocks)), jnp.bfloat16),
        in_specs=[pl.BlockSpec(memory_space=pltpu.SMEM)]
        + [pl.BlockSpec(memory_space=pltpu.VMEM)] * len(blocks),
        out_specs=pl.BlockSpec(memory_space=pltpu.VMEM),
        cost_estimate=pl.CostEstimate(
            flops=0, bytes_accessed=4 * rows * columns * len(blocks), transcendentals=0
        ),
        name="place",
    )(info, *blocks)


def gather_weights(shard):
    owners = lax.axis_size("dp")
    me = lax.axis_index("dp")
    ring = owners // 2
    place_, side = me // 2, me % 2

    def moved(block, step):
        perm = [(o, (o // 2 + step) % ring * 2 + o % 2) for o in range(owners)]
        return lax.ppermute(block, "dp", perm)

    def swapped(block):
        return lax.ppermute(block, "dp", [(o, o ^ 1) for o in range(owners)])

    held = [(place_, shard)]
    ahead, back = shard, shard
    for step in range(1, ring // 2 + 1):
        ahead = moved(ahead, 1)
        held.append(((place_ - step) % ring, ahead))
        if step <= (ring - 1) // 2:
            back = moved(back, -1)
            held.append(((place_ + step) % ring, back))
    blocks = []
    for where, block in held:
        blocks.append((where * 2 + side, block))
        blocks.append((where * 2 + 1 - side, swapped(block)))
    return blocks


def body(
    queries,
    hit_keys,
    hit_values,
    hit_counts,
    master_weight,
    first_moment,
    second_moment,
    gradient,
    owner_bucket,
):
    groups = lax.axis_size("seq")
    chips = groups // 2
    me = lax.axis_index("seq")
    chip, core = me // 2, me % 2
    query, key, value = queries[0], hit_keys[0], hit_values[0]
    rows, width = query.shape
    wide = width // groups

    def to_same(array, step):
        perm = [(s, (s // 2 + step) % chips * 2 + s % 2) for s in range(groups)]
        return lax.ppermute(array, "seq", perm)

    def to_cross(array, step):
        perm = [(s, (s // 2 + step) % chips * 2 + 1 - s % 2) for s in range(groups)]
        return lax.ppermute(array, "seq", perm)

    def to_sibling(array):
        return lax.ppermute(array, "seq", [(s, s ^ 1) for s in range(groups)])

    def cut(array, group):
        return lax.dynamic_slice_in_dim(array, group * wide, wide, 1)

    def pair(group):
        return jnp.stack([cut(key, group), cut(value, group)])

    sibling = me ^ 1
    pairs, sources = [pair(me), to_sibling(pair(sibling))], [me, sibling]
    asked = [[cut(query, me), to_sibling(cut(query, sibling))]]
    for step in range(1, chips):
        target, source = (chip + step) % chips, (chip - step) % chips
        pairs.append(to_same(pair(target * 2 + core), step))
        pairs.append(to_cross(pair(target * 2 + 1 - core), step))
        sources += [source * 2 + core, source * 2 + 1 - core]
        asked.append(
            [
                to_same(cut(query, target * 2 + core), step),
                to_cross(cut(query, target * 2 + 1 - core), step),
            ]
        )
    new_master, new_first, new_second = adam_update(
        master_weight, first_moment, second_moment, gradient
    )
    weights = gather_weights(new_master[0].astype(jnp.bfloat16))

    info = jnp.stack([hit_counts[0]] + sources).astype(jnp.int32)
    attended = [attend(info, blocks, pairs) for blocks in asked]
    spread = [attended] + [[to_same(a, step) for a in attended] for step in range(1, chips)]
    beside = [[to_sibling(a) for a in row] for row in spread]

    owner_ids = jnp.stack([owner for owner, _ in weights])
    bucket = jnp.take(owner_bucket, owner_ids)
    depth = weights[0][1].shape[0]
    parts = wide // depth if wide >= depth else 1
    group, part = bucket // parts, bucket % parts
    slot = (chip - group // 2) % chips * 2 + (group % 2 - core) % 2
    where = (slot * parts + part).astype(jnp.int32)
    blocks = [block for _, block in weights]

    columns = [None] * groups
    for e in list(range(1, chips)) + [0]:
        att = []
        for d in range(chips):
            att += [spread[d][(e - d) % chips], beside[d][(e - d) % chips]]
        out = project(where, att, blocks)
        if e == 0:
            columns[0], columns[1] = out[0], to_sibling(out[1])
        else:
            columns[2 * e] = to_same(out[0], chips - e)
            columns[2 * e + 1] = to_cross(out[1], chips - e)
    order = []
    for e in range(chips):
        other = (chip + e) % chips
        order += [other * 2 + core, other * 2 + 1 - core]
    projected = place(jnp.stack(order).astype(jnp.int32), columns)[None]
    return (projected, new_master, new_first, new_second)


def solution(mesh):
    return jax.shard_map(
        body,
        mesh=mesh,
        in_specs=(
            P("dp", "seq", None),
            P("dp", "seq", None),
            P("dp", "seq", None),
            P("dp"),
            P("dp", None, "seq"),
            P("dp", None, "seq"),
            P("dp", None, "seq"),
            P("dp", None, "seq"),
            P(),
        ),
        out_specs=(
            P("dp", "seq", None),
            P("dp", None, "seq"),
            P("dp", None, "seq"),
            P("dp", None, "seq"),
        ),
        check_vma=False,
    )
```

```python
import functools
import math

import jax
import jax.numpy as jnp
from jax import lax
from jax.experimental import pallas as pl
from jax.experimental.pallas import tpu as pltpu
from jax.sharding import PartitionSpec as P

HEAD_DIM = 128

beta_one = 0.9
beta_two = 0.999
learn_rate = 0.003
weight_decay = 0.1
epsilon = 1e-08
step_count = 10.0


def adam_update(master_weight, first_moment, second_moment, gradient):
    new_first = beta_one * first_moment + (1.0 - beta_one) * gradient
    new_second = beta_two * second_moment + (1.0 - beta_two) * gradient * gradient
    first_hat = new_first / (1.0 - beta_one**step_count)
    second_hat = new_second / (1.0 - beta_two**step_count)
    new_master = master_weight - learn_rate * (
        first_hat / (jnp.sqrt(second_hat) + epsilon) + weight_decay * master_weight
    )
    return (new_master, new_first, new_second)


ATTEND_US = 3
PROJECT_US = 2

SMALL = pltpu.CompilerParams(vmem_limit_bytes=16 * 1024 * 1024)
IN_VMEM = pl.BlockSpec(memory_space=pltpu.VMEM)
IN_SMEM = pl.BlockSpec(memory_space=pltpu.SMEM)


def estimate(micros):
    return pl.CostEstimate(flops=0, bytes_accessed=int(micros * 3.69e6), transcendentals=0)


def chip_and_core():
    me = lax.axis_index("seq")
    return lax.shift_right_logical(me, 1), lax.bitwise_and(me, 1)


def turned(position, step, size):
    moved = position + step
    return jnp.where(moved >= size, moved - size, moved)


def cut_kernel(n_arrays, *refs):
    arrays, blocks, sems = refs[:n_arrays], refs[n_arrays:-1], refs[-1]
    chips = len(blocks) // 2
    chip, core = chip_and_core()
    copies = []
    for i, block in enumerate(blocks):
        group = 2 * turned(chip, i // 2, chips) + (core if i % 2 == 0 else 1 - core)
        wide = block.shape[-1]
        lanes = pl.ds(pl.multiple_of(group * wide, wide), wide)
        for j, array in enumerate(arrays):
            target = block if n_arrays == 1 else block.at[j]
            copies.append(pltpu.make_async_copy(array.at[:, lanes], target, sems.at[i, j]))
    for copy in copies:
        copy.start()
    for copy in copies:
        copy.wait()


def cut(*arrays):
    groups = lax.axis_size("seq")
    rows, width = arrays[0].shape
    shape = (rows, width // groups)
    if len(arrays) > 1:
        shape = (len(arrays),) + shape
    return pl.pallas_call(
        functools.partial(cut_kernel, len(arrays)),
        out_shape=[jax.ShapeDtypeStruct(shape, jnp.bfloat16)] * groups,
        in_specs=[pl.BlockSpec(memory_space=pl.ANY)] * len(arrays),
        out_specs=[pl.BlockSpec(memory_space=pl.ANY)] * groups,
        scratch_shapes=[pltpu.SemaphoreType.DMA((groups, len(arrays)))],
        compiler_params=SMALL,
        cost_estimate=estimate(1),
        name="cut",
    )(*arrays)


def attend_kernel(n_keys, count_ref, *refs):
    query_refs, pair_refs = refs[:2], refs[2 : 2 + n_keys]
    out_ref, keys, values = refs[2 + n_keys :]
    rows, wide = query_refs[0].shape
    chips = n_keys // 2
    chip, core = chip_and_core()
    columns = []
    for i, ref in enumerate(pair_refs):
        keys[i * rows : (i + 1) * rows, :] = ref[0]
        values[i * rows : (i + 1) * rows, :] = ref[1]
        source = 2 * turned(chip, (chips - i // 2) % chips, chips) + (core if i % 2 == 0 else 1 - core)
        columns.append(source * rows + lax.broadcasted_iota(jnp.int32, (1, rows), 1))
    valid = jnp.concatenate(columns, axis=1) < count_ref[0]
    factor = HEAD_DIM ** (-0.5) * math.log2(math.e)
    for block, query_ref in enumerate(query_refs):
        for head in range(wide // HEAD_DIM):
            lanes = slice(head * HEAD_DIM, (head + 1) * HEAD_DIM)
            scores = lax.dot_general(
                query_ref[:, lanes],
                keys[:, lanes],
                (((1,), (1,)), ((), ())),
                preferred_element_type=jnp.float32,
            )
            scores = jnp.where(valid, scores, -1e30)
            top = jnp.max(scores, axis=1, keepdims=True)
            expo = jnp.exp2((scores - top) * factor)
            total = jnp.sum(expo, axis=1, keepdims=True)
            weights = (expo * (1.0 / total)).astype(jnp.bfloat16)
            out_ref[block, :, lanes] = jnp.dot(
                weights, values[:, lanes], preferred_element_type=jnp.float32
            ).astype(jnp.bfloat16)


def attend(counts, query_blocks, pairs):
    rows, wide = query_blocks[0].shape
    n_keys = len(pairs)
    return pl.pallas_call(
        functools.partial(attend_kernel, n_keys),
        out_shape=jax.ShapeDtypeStruct((2, rows, wide), jnp.bfloat16),
        in_specs=[IN_SMEM] + [IN_VMEM] * (2 + n_keys),
        out_specs=IN_VMEM,
        scratch_shapes=[pltpu.VMEM((n_keys * rows, wide), jnp.bfloat16)] * 2,
        compiler_params=SMALL,
        cost_estimate=estimate(ATTEND_US),
        name="attend",
    )(counts, *query_blocks, *pairs)


def project_kernel(n_att, steps, bucket_ref, *refs):
    att_refs, weight_refs = refs[:n_att], refs[n_att : n_att + 2 * len(steps)]
    out_ref, other_ref, held = refs[n_att + 2 * len(steps) :]
    _, rows, wide = att_refs[0].shape
    depth = weight_refs[0].shape[0]
    parts = wide // depth
    chip, core = chip_and_core()
    owner = lax.axis_index("dp")
    ring = lax.axis_size("dp") // 2
    spot, side = lax.shift_right_logical(owner, 1), lax.bitwise_and(owner, 1)
    for slot, ref in enumerate(att_refs):
        for block in range(2):
            for part in range(parts):
                held[slot * parts + part, block * rows : (block + 1) * rows, :] = ref[
                    block ^ (slot % 2), :, part * depth : (part + 1) * depth
                ]
    total = None
    for i, ref in enumerate(weight_refs):
        from_owner = 2 * turned(spot, steps[i // 2], ring) + (side if i % 2 == 0 else 1 - side)
        bucket = bucket_ref[from_owner]
        group, part = lax.div(bucket, parts), lax.rem(bucket, parts)
        group_chip, group_core = lax.shift_right_logical(group, 1), lax.bitwise_and(group, 1)
        back = chip - group_chip
        back = jnp.where(back < 0, back + n_att // 2, back)
        slot = 2 * back + lax.bitwise_xor(group_core, core)
        term = jnp.dot(held[slot * parts + part], ref[...], preferred_element_type=jnp.float32)
        total = term if total is None else total + term
    total = total.astype(jnp.bfloat16)
    out_ref[...] = total[:rows]
    other_ref[...] = total[rows:]


def project(owner_bucket, att, steps, weights):
    _, rows, wide = att[0].shape
    depth, columns = weights[0].shape
    return pl.pallas_call(
        functools.partial(project_kernel, len(att), steps),
        out_shape=[jax.ShapeDtypeStruct((rows, columns), jnp.bfloat16)] * 2,
        in_specs=[IN_SMEM] + [IN_VMEM] * (len(att) + len(weights)),
        out_specs=[IN_VMEM] * 2,
        scratch_shapes=[pltpu.VMEM((len(att) * wide // depth, 2 * rows, depth), jnp.bfloat16)],
        compiler_params=SMALL,
        cost_estimate=estimate(PROJECT_US),
        name="project",
    )(owner_bucket, *att, *weights)


def place_kernel(n, *refs):
    out_ref = refs[n]
    columns = refs[0].shape[1]
    chip, core = chip_and_core()
    for i in range(n):
        group = 2 * turned(chip, i // 2, n // 2) + (core if i % 2 == 0 else 1 - core)
        out_ref[:, pl.ds(pl.multiple_of(group * columns, columns), columns)] = refs[i][...]


def place(blocks):
    rows, columns = blocks[0].shape
    return pl.pallas_call(
        functools.partial(place_kernel, len(blocks)),
        out_shape=jax.ShapeDtypeStruct((rows, columns * len(blocks)), jnp.bfloat16),
        in_specs=[IN_VMEM] * len(blocks),
        out_specs=IN_VMEM,
        compiler_params=SMALL,
        cost_estimate=estimate(1),
        name="place",
    )(*blocks)


def gather_weights(shard):
    owners = lax.axis_size("dp")
    ring = owners // 2

    def moved(block, step):
        perm = [(o, (o // 2 + step) % ring * 2 + o % 2) for o in range(owners)]
        return lax.ppermute(block, "dp", perm)

    def swapped(block):
        return lax.ppermute(block, "dp", [(o, o ^ 1) for o in range(owners)])

    steps, held = [0], [shard]
    ahead, back = shard, shard
    for step in range(1, ring // 2 + 1):
        ahead = moved(ahead, 1)
        held.append(ahead)
        steps.append((-step) % ring)
        if step <= (ring - 1) // 2:
            back = moved(back, -1)
            held.append(back)
            steps.append(step)
    blocks = []
    for block in held:
        blocks += [block, swapped(block)]
    return steps, blocks


def body(
    queries,
    hit_keys,
    hit_values,
    hit_counts,
    master_weight,
    first_moment,
    second_moment,
    gradient,
    owner_bucket,
):
    groups = lax.axis_size("seq")
    chips = groups // 2

    def to_same(array, step):
        perm = [(s, (s // 2 + step) % chips * 2 + s % 2) for s in range(groups)]
        return lax.ppermute(array, "seq", perm)

    def to_cross(array, step):
        perm = [(s, (s // 2 + step) % chips * 2 + 1 - s % 2) for s in range(groups)]
        return lax.ppermute(array, "seq", perm)

    def to_sibling(array):
        return lax.ppermute(array, "seq", [(s, s ^ 1) for s in range(groups)])

    def exchanged(blocks):
        got = [blocks[0], to_sibling(blocks[1])]
        for step in range(1, chips):
            got += [to_same(blocks[2 * step], step), to_cross(blocks[2 * step + 1], step)]
        return got

    pairs = exchanged(cut(hit_keys[0], hit_values[0]))
    new_master, new_first, new_second = adam_update(
        master_weight, first_moment, second_moment, gradient
    )
    steps, weights = gather_weights(new_master[0].astype(jnp.bfloat16))
    asked = exchanged(cut(queries[0]))

    attended = [attend(hit_counts, asked[2 * e : 2 * e + 2], pairs) for e in range(chips)]
    spread = [attended] + [[to_same(a, step) for a in attended] for step in range(1, chips)]
    beside = [[to_sibling(a) for a in row] for row in spread]

    columns = [None] * groups
    for e in list(range(1, chips)) + [0]:
        att = []
        for d in range(chips):
            att += [spread[d][(e - d) % chips], beside[d][(e - d) % chips]]
        out, other = project(owner_bucket, att, steps, weights)
        if e == 0:
            columns[0], columns[1] = out, to_sibling(other)
        else:
            columns[2 * e] = to_same(out, chips - e)
            columns[2 * e + 1] = to_cross(other, chips - e)
    projected = place(columns)[None]
    return (projected, new_master, new_first, new_second)


def solution(mesh):
    return jax.shard_map(
        body,
        mesh=mesh,
        in_specs=(
            P("dp", "seq", None),
            P("dp", "seq", None),
            P("dp", "seq", None),
            P("dp"),
            P("dp", None, "seq"),
            P("dp", None, "seq"),
            P("dp", None, "seq"),
            P("dp", None, "seq"),
            P(),
        ),
        out_specs=(
            P("dp", "seq", None),
            P("dp", None, "seq"),
            P("dp", None, "seq"),
            P("dp", None, "seq"),
        ),
        check_vma=False,
    )
```

```python
import functools
import math

import jax
import jax.numpy as jnp
from jax import lax
from jax.experimental import pallas as pl
from jax.experimental.pallas import tpu as pltpu
from jax.sharding import PartitionSpec as P

HEAD_DIM = 128

beta_one = 0.9
beta_two = 0.999
learn_rate = 0.003
weight_decay = 0.1
epsilon = 1e-08
step_count = 10.0


def adam_update(master_weight, first_moment, second_moment, gradient):
    new_first = beta_one * first_moment + (1.0 - beta_one) * gradient
    new_second = beta_two * second_moment + (1.0 - beta_two) * gradient * gradient
    first_hat = new_first / (1.0 - beta_one**step_count)
    second_hat = new_second / (1.0 - beta_two**step_count)
    new_master = master_weight - learn_rate * (
        first_hat / (jnp.sqrt(second_hat) + epsilon) + weight_decay * master_weight
    )
    return (new_master, new_first, new_second)


ATTEND_US = 3
HALF_STEPS = 2
PROJECT_US = 2

SMALL = pltpu.CompilerParams(vmem_limit_bytes=16 * 1024 * 1024)
IN_VMEM = pl.BlockSpec(memory_space=pltpu.VMEM)
IN_SMEM = pl.BlockSpec(memory_space=pltpu.SMEM)


def estimate(micros):
    return pl.CostEstimate(flops=0, bytes_accessed=int(micros * 3.69e6), transcendentals=0)


def chip_and_core():
    me = lax.axis_index("seq")
    return lax.shift_right_logical(me, 1), lax.bitwise_and(me, 1)


def turned(position, step, size):
    moved = position + step
    return jnp.where(moved >= size, moved - size, moved)


def after(value, *others):
    return lax.optimization_barrier((value,) + others)[0]


def half_kernel(master_ref, first_ref, second_ref, gradient_ref, half_ref):
    new_master, _, _ = adam_update(
        master_ref[...], first_ref[...], second_ref[...], gradient_ref[...]
    )
    half_ref[...] = new_master.astype(jnp.bfloat16)


def half(master_weight, first_moment, second_moment, gradient):
    depth, columns = master_weight.shape
    rows = depth // HALF_STEPS
    spec = pl.BlockSpec((rows, columns), lambda i: (i, 0))
    return pl.pallas_call(
        half_kernel,
        grid=(HALF_STEPS,),
        out_shape=jax.ShapeDtypeStruct((depth, columns), jnp.bfloat16),
        in_specs=[spec] * 4,
        out_specs=spec,
        compiler_params=SMALL,
        cost_estimate=estimate(1),
        name="half",
    )(*[
        pltpu.with_memory_space_constraint(array, pltpu.HBM)
        for array in (master_weight, first_moment, second_moment, gradient)
    ])


def cut_kernel(query, key, value, *refs):
    blocks, sems = refs[:-1], refs[-1]
    chips = (len(blocks) - 2) // 3 + 1
    wide = blocks[0].shape[-1]
    chip, core = chip_and_core()
    copies = []

    def copy(array, step, crossed, target):
        group = 2 * turned(chip, step, chips) + (1 - core if crossed else core)
        lanes = pl.ds(pl.multiple_of(group * wide, wide), wide)
        copies.append(pltpu.make_async_copy(array.at[:, lanes], target, sems.at[len(copies)]))

    for step in range(1, chips):
        for crossed in range(2):
            for i, array in enumerate((key, value)):
                copy(array, step, crossed, blocks[3 * step - 1 + crossed].at[i])
    for crossed in (1, 0):
        for i, array in enumerate((query, key, value)):
            copy(array, 0, crossed, blocks[crossed].at[i])
    for step in range(1, chips):
        for crossed in range(2):
            copy(query, step, crossed, blocks[3 * step + 1].at[crossed])
    for one in copies:
        one.start()
    for one in copies:
        one.wait()


def cut(*arrays):
    groups = lax.axis_size("seq")
    rows, width = arrays[0].shape
    counts = [3, 3] + [2] * (3 * (groups // 2 - 1))
    return pl.pallas_call(
        cut_kernel,
        out_shape=[
            jax.ShapeDtypeStruct((n, rows, width // groups), jnp.bfloat16) for n in counts
        ],
        in_specs=[pl.BlockSpec(memory_space=pl.ANY)] * 3,
        out_specs=[IN_VMEM] * len(counts),
        scratch_shapes=[pltpu.SemaphoreType.DMA((3 * groups,))],
        compiler_params=SMALL,
        cost_estimate=estimate(1),
        name="cut",
    )(*[pltpu.with_memory_space_constraint(array, pltpu.HBM) for array in arrays])


def attend_kernel(n_pairs, picks, count_ref, *refs):
    pair_refs = refs[:n_pairs]
    out_ref, keys, values = refs[-3:]
    _, rows, wide = out_ref.shape
    chips = n_pairs // 2
    chip, core = chip_and_core()
    columns = []
    for i, ref in enumerate(pair_refs):
        keys[i * rows : (i + 1) * rows, :] = ref[ref.shape[0] - 2]
        values[i * rows : (i + 1) * rows, :] = ref[ref.shape[0] - 1]
        source = 2 * turned(chip, (chips - i // 2) % chips, chips) + (core if i % 2 == 0 else 1 - core)
        columns.append(source * rows + lax.broadcasted_iota(jnp.int32, (1, rows), 1))
    valid = jnp.concatenate(columns, axis=1) < count_ref[0]
    factor = HEAD_DIM ** (-0.5) * math.log2(math.e)
    for block, (at, index) in enumerate(picks):
        for head in range(wide // HEAD_DIM):
            lanes = slice(head * HEAD_DIM, (head + 1) * HEAD_DIM)
            scores = lax.dot_general(
                refs[at][index, :, lanes],
                keys[:, lanes],
                (((1,), (1,)), ((), ())),
                preferred_element_type=jnp.float32,
            )
            scores = jnp.where(valid, scores, -1e30)
            top = jnp.max(scores, axis=1, keepdims=True)
            expo = jnp.exp2((scores - top) * factor)
            total = jnp.sum(expo, axis=1, keepdims=True)
            mixed = jnp.dot(
                expo.astype(jnp.bfloat16), values[:, lanes], preferred_element_type=jnp.float32
            )
            out_ref[block, :, lanes] = (mixed * (1.0 / total)).astype(jnp.bfloat16)


def attend(counts, pairs, queries=()):
    _, rows, wide = pairs[0].shape
    n_pairs = len(pairs)
    picks = ((n_pairs, 0), (n_pairs + 1, 1)) if queries else ((0, 0), (1, 0))
    return pl.pallas_call(
        functools.partial(attend_kernel, n_pairs, picks),
        out_shape=jax.ShapeDtypeStruct((2, rows, wide), jnp.bfloat16),
        in_specs=[IN_SMEM] + [IN_VMEM] * (n_pairs + len(queries)),
        out_specs=IN_VMEM,
        scratch_shapes=[pltpu.VMEM((n_pairs * rows, wide), jnp.bfloat16)] * 2,
        compiler_params=SMALL,
        cost_estimate=estimate(ATTEND_US),
        name="attend",
    )(counts, *pairs, *queries)


def project_kernel(n_att, steps, bucket_ref, *refs):
    att_refs, weight_refs = refs[:n_att], refs[n_att : n_att + 2 * len(steps)]
    out_ref, other_ref, held = refs[n_att + 2 * len(steps) :]
    _, rows, wide = att_refs[0].shape
    depth = weight_refs[0].shape[0]
    parts = wide // depth
    chip, core = chip_and_core()
    owner = lax.axis_index("dp")
    ring = lax.axis_size("dp") // 2
    spot, side = lax.shift_right_logical(owner, 1), lax.bitwise_and(owner, 1)
    for slot, ref in enumerate(att_refs):
        for block in range(2):
            for part in range(parts):
                held[slot * parts + part, block * rows : (block + 1) * rows, :] = ref[
                    block ^ (slot % 2), :, part * depth : (part + 1) * depth
                ]
    total = None
    for i, ref in enumerate(weight_refs):
        from_owner = 2 * turned(spot, steps[i // 2], ring) + (side if i % 2 == 0 else 1 - side)
        bucket = bucket_ref[from_owner]
        group, part = lax.div(bucket, parts), lax.rem(bucket, parts)
        group_chip, group_core = lax.shift_right_logical(group, 1), lax.bitwise_and(group, 1)
        back = chip - group_chip
        back = jnp.where(back < 0, back + n_att // 2, back)
        slot = 2 * back + lax.bitwise_xor(group_core, core)
        term = jnp.dot(held[slot * parts + part], ref[...], preferred_element_type=jnp.float32)
        total = term if total is None else total + term
    total = total.astype(jnp.bfloat16)
    out_ref[...] = total[:rows]
    other_ref[...] = total[rows:]


def project(owner_bucket, att, steps, weights):
    _, rows, wide = att[0].shape
    depth, columns = weights[0].shape
    return pl.pallas_call(
        functools.partial(project_kernel, len(att), steps),
        out_shape=[jax.ShapeDtypeStruct((rows, columns), jnp.bfloat16)] * 2,
        in_specs=[IN_SMEM] + [IN_VMEM] * (len(att) + len(weights)),
        out_specs=[IN_VMEM] * 2,
        scratch_shapes=[pltpu.VMEM((len(att) * wide // depth, 2 * rows, depth), jnp.bfloat16)],
        compiler_params=SMALL,
        cost_estimate=estimate(PROJECT_US),
        name="project",
    )(owner_bucket, *att, *weights)


def place_kernel(n, *refs):
    out_ref = refs[n]
    columns = refs[0].shape[1]
    chip, core = chip_and_core()
    for i in range(n):
        group = 2 * turned(chip, i // 2, n // 2) + (core if i % 2 == 0 else 1 - core)
        out_ref[:, pl.ds(pl.multiple_of(group * columns, columns), columns)] = refs[i][...]


def place(blocks):
    rows, columns = blocks[0].shape
    return pl.pallas_call(
        functools.partial(place_kernel, len(blocks)),
        out_shape=jax.ShapeDtypeStruct((rows, columns * len(blocks)), jnp.bfloat16),
        in_specs=[IN_VMEM] * len(blocks),
        out_specs=IN_VMEM,
        compiler_params=SMALL,
        cost_estimate=estimate(1),
        name="place",
    )(*blocks)


def gather_weights(shard, first):
    owners = lax.axis_size("dp")
    ring = owners // 2

    def moved(block, step, name):
        perm = [(o, (o // 2 + step) % ring * 2 + o % 2) for o in range(owners)]
        with jax.named_scope(name):
            return lax.ppermute(block, "dp", perm)

    def swapped(block, name):
        with jax.named_scope(name):
            return lax.ppermute(block, "dp", [(o, o ^ 1) for o in range(owners)])

    steps, held, names = [0], [shard], ["swap_own"]
    ahead, back = shard, shard
    for step in range(1, ring // 2 + 1):
        ahead = moved(ahead, 1, f"ahead{step}")
        held.append(ahead)
        names.append(f"swap_ahead{step}")
        steps.append((-step) % ring)
        if step <= (ring - 1) // 2:
            back = moved(back, -1, f"back{step}")
            held.append(back)
            names.append(f"swap_back{step}")
            steps.append(step)
    blocks = [shard, swapped(after(shard, first), names[0])]
    for block, name in zip(held[1:], names[1:]):
        blocks += [block, swapped(block, name)]
    return steps, blocks, held[1:]


def body(
    queries,
    hit_keys,
    hit_values,
    hit_counts,
    master_weight,
    first_moment,
    second_moment,
    gradient,
    owner_bucket,
):
    groups = lax.axis_size("seq")
    chips = groups // 2

    def to_same(array, step, name):
        perm = [(s, (s // 2 + step) % chips * 2 + s % 2) for s in range(groups)]
        with jax.named_scope(name):
            return lax.ppermute(array, "seq", perm)

    def to_cross(array, step, name):
        perm = [(s, (s // 2 + step) % chips * 2 + 1 - s % 2) for s in range(groups)]
        with jax.named_scope(name):
            return lax.ppermute(array, "seq", perm)

    def to_sibling(array, name):
        with jax.named_scope(name):
            return lax.ppermute(array, "seq", [(s, s ^ 1) for s in range(groups)])

    master, first = master_weight[0], first_moment[0]
    second, grad = second_moment[0], gradient[0]

    own, other, *rest = cut(queries[0], hit_keys[0], hit_values[0])
    rounded = half(master, first, second, grad)
    sibling = to_sibling(other, "sibling")
    steps, weights, ring = gather_weights(rounded, sibling)
    pairs, asked = [own, sibling], [()]
    for step in range(1, chips):
        same, cross, queries_for = rest[3 * step - 3 : 3 * step]
        pairs += [
            to_same(same, step, "pairs_same"),
            to_cross(after(cross, sibling), step, "pairs_cross"),
        ]
        here = to_same(after(queries_for, pairs[-2], rounded), step, "queries")
        asked.append((here, to_sibling(here, "queries_sibling")))

    attended = [attend(hit_counts, [after(own, ring[0], ring[1], weights[1])] + pairs[1:])]
    for here, beside in asked[1:]:
        attended.append(attend(hit_counts, pairs, (after(here, attended[-1], ring[2], weights[3]), beside)))
    pass
    spread = [attended] + [
        [to_same(a, step, f"attended{e}_same") for e, a in enumerate(attended)]
        for step in range(1, chips)
    ]
    beside = [
        [to_sibling(after(a, spread[1][0], weights[5]), f"spread{d}_{e}_sibling") for e, a in enumerate(row)]
        for d, row in enumerate(spread)
    ]

    columns = [None] * groups
    for e in list(range(1, chips)) + [0]:
        att = []
        for d in range(chips):
            att += [spread[d][(e - d) % chips], beside[d][(e - d) % chips]]
        if e == 0:
            att[0] = after(att[0], out)
        out, other = project(owner_bucket, att, steps, weights)
        if e == 0:
            columns[0], columns[1] = out, to_sibling(other, "out_sibling")
        else:
            columns[2 * e] = to_same(out, chips - e, "out_same")
            columns[2 * e + 1] = to_cross(other, chips - e, "out_cross")
    projected = place(columns)[None]
    new_master, new_first, new_second = adam_update(*lax.optimization_barrier(
        (master_weight, first_moment, second_moment, gradient, columns[0]))[:4])
    return (projected, new_master, new_first, new_second)


def solution(mesh):
    return jax.shard_map(
        body,
        mesh=mesh,
        in_specs=(
            P("dp", "seq", None),
            P("dp", "seq", None),
            P("dp", "seq", None),
            P("dp"),
            P("dp", None, "seq"),
            P("dp", None, "seq"),
            P("dp", None, "seq"),
            P("dp", None, "seq"),
            P(),
        ),
        out_specs=(
            P("dp", "seq", None),
            P("dp", None, "seq"),
            P("dp", None, "seq"),
            P("dp", None, "seq"),
        ),
        check_vma=False,
    )
```

```python
import functools
import math

import jax
import jax.numpy as jnp
from jax import lax
from jax.experimental import pallas as pl
from jax.experimental.pallas import tpu as pltpu
from jax.sharding import PartitionSpec as P

HEAD_DIM = 128

beta_one = 0.9
beta_two = 0.999
learn_rate = 0.003
weight_decay = 0.1
epsilon = 1e-08
step_count = 10.0


def adam_update(master_weight, first_moment, second_moment, gradient):
    new_first = beta_one * first_moment + (1.0 - beta_one) * gradient
    new_second = beta_two * second_moment + (1.0 - beta_two) * gradient * gradient
    first_hat = new_first / (1.0 - beta_one**step_count)
    second_hat = new_second / (1.0 - beta_two**step_count)
    new_master = master_weight - learn_rate * (
        first_hat / (jnp.sqrt(second_hat) + epsilon) + weight_decay * master_weight
    )
    return (new_master, new_first, new_second)


ATTEND_US = 3
HALF_STEPS = 2
PROJECT_US = 2

FIRST = {
    "half": ["cut"],
    "queries1_same": ["pairs1_same"],
    "queries1_cross": ["pairs1_same", "sibling", "pairs1_cross"],
    "attend0": ["swap_own"],
    "attend1": ["attend0", "ahead3"],
    "attended1_to1": ["swap_ahead1"],
    "sibling0_for1": ["attended0_to1"],
    "sibling1_for1": ["swap_ahead3"],
    "sibling0_for0": ["attended0_to1"],
    "project0": ["project1"],
    "states": ["attended0_to1"],
}

SMALL = pltpu.CompilerParams(vmem_limit_bytes=16 * 1024 * 1024)
IN_VMEM = pl.BlockSpec(memory_space=pltpu.VMEM)
IN_SMEM = pl.BlockSpec(memory_space=pltpu.SMEM)


def estimate(micros):
    return pl.CostEstimate(flops=0, bytes_accessed=int(micros * 3.69e6), transcendentals=0)


def chip_and_core():
    me = lax.axis_index("seq")
    return lax.shift_right_logical(me, 1), lax.bitwise_and(me, 1)


def turned(position, step, size):
    moved = position + step
    return jnp.where(moved >= size, moved - size, moved)


class Seen:
    def __init__(self):
        self.values = {}

    def add(self, name, value):
        self.values[name] = value
        return value

    def after(self, name, value):
        others = [self.values[n] for n in FIRST.get(name, ()) if n in self.values]
        return lax.optimization_barrier((value, *others))[0] if others else value

    def permute(self, name, array, axis, perm):
        array = self.after(name, array)
        with jax.named_scope(name):
            return self.add(name, lax.ppermute(array, axis, perm))


def half_kernel(master_ref, first_ref, second_ref, gradient_ref, half_ref):
    new_master, _, _ = adam_update(
        master_ref[...], first_ref[...], second_ref[...], gradient_ref[...]
    )
    half_ref[...] = new_master.astype(jnp.bfloat16)


def half(master_weight, first_moment, second_moment, gradient):
    depth, columns = master_weight.shape
    rows = depth // HALF_STEPS
    spec = pl.BlockSpec((rows, columns), lambda i: (i, 0))
    return pl.pallas_call(
        half_kernel,
        grid=(HALF_STEPS,),
        out_shape=jax.ShapeDtypeStruct((depth, columns), jnp.bfloat16),
        in_specs=[spec] * 4,
        out_specs=spec,
        compiler_params=SMALL,
        cost_estimate=estimate(1),
        name="half",
    )(*[
        pltpu.with_memory_space_constraint(array, pltpu.HBM)
        for array in (master_weight, first_moment, second_moment, gradient)
    ])


def cut_kernel(query, key, value, *refs):
    blocks, sems = refs[:-1], refs[-1]
    chips = (len(blocks) - 2) // 4 + 1
    wide = blocks[0].shape[-1]
    chip, core = chip_and_core()
    copies = []

    def copy(array, step, crossed, target):
        group = 2 * turned(chip, step, chips) + (1 - core if crossed else core)
        lanes = pl.ds(pl.multiple_of(group * wide, wide), wide)
        copies.append(pltpu.make_async_copy(array.at[:, lanes], target, sems.at[len(copies)]))

    for step in range(1, chips):
        for crossed in range(2):
            for i, array in enumerate((key, value)):
                copy(array, step, crossed, blocks[4 * step - 2 + crossed].at[i])
    for crossed in (1, 0):
        for i, array in enumerate((query, key, value)):
            copy(array, 0, crossed, blocks[crossed].at[i])
    for step in range(1, chips):
        for crossed in range(2):
            copy(query, step, crossed, blocks[4 * step + crossed].at[0])
    for one in copies:
        one.start()
    for one in copies:
        one.wait()


def cut(*arrays):
    groups = lax.axis_size("seq")
    rows, width = arrays[0].shape
    counts = [3, 3] + [2, 2, 1, 1] * (groups // 2 - 1)
    return pl.pallas_call(
        cut_kernel,
        out_shape=[
            jax.ShapeDtypeStruct((n, rows, width // groups), jnp.bfloat16) for n in counts
        ],
        in_specs=[pl.BlockSpec(memory_space=pl.ANY)] * 3,
        out_specs=[IN_VMEM] * len(counts),
        scratch_shapes=[pltpu.SemaphoreType.DMA((3 * groups,))],
        compiler_params=SMALL,
        cost_estimate=estimate(1),
        name="cut",
    )(*[pltpu.with_memory_space_constraint(array, pltpu.HBM) for array in arrays])


def attend_kernel(n_pairs, picks, count_ref, *refs):
    pair_refs = refs[:n_pairs]
    out_ref, keys, values = refs[-3:]
    _, rows, wide = out_ref.shape
    chips = n_pairs // 2
    chip, core = chip_and_core()
    columns = []
    for i, ref in enumerate(pair_refs):
        keys[i * rows : (i + 1) * rows, :] = ref[ref.shape[0] - 2]
        values[i * rows : (i + 1) * rows, :] = ref[ref.shape[0] - 1]
        source = 2 * turned(chip, (chips - i // 2) % chips, chips) + (core if i % 2 == 0 else 1 - core)
        columns.append(source * rows + lax.broadcasted_iota(jnp.int32, (1, rows), 1))
    valid = jnp.concatenate(columns, axis=1) < count_ref[0]
    factor = HEAD_DIM ** (-0.5) * math.log2(math.e)
    for block, (at, index) in enumerate(picks):
        for head in range(wide // HEAD_DIM):
            lanes = slice(head * HEAD_DIM, (head + 1) * HEAD_DIM)
            scores = lax.dot_general(
                refs[at][index, :, lanes],
                keys[:, lanes],
                (((1,), (1,)), ((), ())),
                preferred_element_type=jnp.float32,
            )
            scores = jnp.where(valid, scores, -1e30)
            top = jnp.max(scores, axis=1, keepdims=True)
            expo = jnp.exp2((scores - top) * factor)
            total = jnp.sum(expo, axis=1, keepdims=True)
            mixed = jnp.dot(
                expo.astype(jnp.bfloat16), values[:, lanes], preferred_element_type=jnp.float32
            )
            out_ref[block, :, lanes] = (mixed * (1.0 / total)).astype(jnp.bfloat16)


def attend(counts, pairs, queries=()):
    _, rows, wide = pairs[0].shape
    n_pairs = len(pairs)
    picks = ((n_pairs, 0), (n_pairs + 1, 0)) if queries else ((0, 0), (1, 0))
    return pl.pallas_call(
        functools.partial(attend_kernel, n_pairs, picks),
        out_shape=jax.ShapeDtypeStruct((2, rows, wide), jnp.bfloat16),
        in_specs=[IN_SMEM] + [IN_VMEM] * (n_pairs + len(queries)),
        out_specs=IN_VMEM,
        scratch_shapes=[pltpu.VMEM((n_pairs * rows, wide), jnp.bfloat16)] * 2,
        compiler_params=SMALL,
        cost_estimate=estimate(ATTEND_US),
        name="attend",
    )(counts, *pairs, *queries)


def project_kernel(n_att, steps, bucket_ref, *refs):
    att_refs, weight_refs = refs[:n_att], refs[n_att : n_att + 2 * len(steps)]
    out_ref, other_ref, held = refs[n_att + 2 * len(steps) :]
    _, rows, wide = att_refs[0].shape
    depth = weight_refs[0].shape[0]
    parts = wide // depth
    chip, core = chip_and_core()
    owner = lax.axis_index("dp")
    ring = lax.axis_size("dp") // 2
    spot, side = lax.shift_right_logical(owner, 1), lax.bitwise_and(owner, 1)
    for slot, ref in enumerate(att_refs):
        for block in range(2):
            for part in range(parts):
                held[slot * parts + part, block * rows : (block + 1) * rows, :] = ref[
                    block ^ (slot % 2), :, part * depth : (part + 1) * depth
                ]
    total = None
    for i, ref in enumerate(weight_refs):
        from_owner = 2 * turned(spot, steps[i // 2], ring) + (side if i % 2 == 0 else 1 - side)
        bucket = bucket_ref[from_owner]
        group, part = lax.div(bucket, parts), lax.rem(bucket, parts)
        group_chip, group_core = lax.shift_right_logical(group, 1), lax.bitwise_and(group, 1)
        back = chip - group_chip
        back = jnp.where(back < 0, back + n_att // 2, back)
        slot = 2 * back + lax.bitwise_xor(group_core, core)
        term = jnp.dot(held[slot * parts + part], ref[...], preferred_element_type=jnp.float32)
        total = term if total is None else total + term
    total = total.astype(jnp.bfloat16)
    out_ref[...] = total[:rows]
    other_ref[...] = total[rows:]


def project(owner_bucket, att, steps, weights):
    _, rows, wide = att[0].shape
    depth, columns = weights[0].shape
    return pl.pallas_call(
        functools.partial(project_kernel, len(att), steps),
        out_shape=[jax.ShapeDtypeStruct((rows, columns), jnp.bfloat16)] * 2,
        in_specs=[IN_SMEM] + [IN_VMEM] * (len(att) + len(weights)),
        out_specs=[IN_VMEM] * 2,
        scratch_shapes=[pltpu.VMEM((len(att) * wide // depth, 2 * rows, depth), jnp.bfloat16)],
        compiler_params=SMALL,
        cost_estimate=estimate(PROJECT_US),
        name="project",
    )(owner_bucket, *att, *weights)


def place_kernel(n, *refs):
    out_ref = refs[n]
    columns = refs[0].shape[1]
    chip, core = chip_and_core()
    for i in range(n):
        group = 2 * turned(chip, i // 2, n // 2) + (core if i % 2 == 0 else 1 - core)
        out_ref[:, pl.ds(pl.multiple_of(group * columns, columns), columns)] = refs[i][...]


def place(blocks):
    rows, columns = blocks[0].shape
    return pl.pallas_call(
        functools.partial(place_kernel, len(blocks)),
        out_shape=jax.ShapeDtypeStruct((rows, columns * len(blocks)), jnp.bfloat16),
        in_specs=[IN_VMEM] * len(blocks),
        out_specs=IN_VMEM,
        compiler_params=SMALL,
        cost_estimate=estimate(1),
        name="place",
    )(*blocks)


def gather_weights(seen, shard):
    owners = lax.axis_size("dp")
    ring = owners // 2

    def moved(block, step, name):
        perm = [(o, (o // 2 + step) % ring * 2 + o % 2) for o in range(owners)]
        return seen.permute(name, block, "dp", perm)

    held = [(0, shard, "swap_own")]
    ahead = back = shard
    for step in range(1, ring // 2 + 1):
        ahead = moved(ahead, 1, f"ahead{step}")
        held.append((-step % ring, ahead, f"swap_ahead{step}"))
        if step <= (ring - 1) // 2:
            back = moved(back, -1, f"back{step}")
            held.append((step, back, f"swap_back{step}"))
    blocks = []
    for _, block, name in held:
        swapped = seen.permute(name, block, "dp", [(o, o ^ 1) for o in range(owners)])
        blocks += [block, swapped]
    return [step for step, _, _ in held], blocks


def body(
    queries,
    hit_keys,
    hit_values,
    hit_counts,
    master_weight,
    first_moment,
    second_moment,
    gradient,
    owner_bucket,
):
    groups = lax.axis_size("seq")
    chips = groups // 2
    seen = Seen()

    def to_same(name, array, step):
        perm = [(s, (s // 2 + step) % chips * 2 + s % 2) for s in range(groups)]
        return seen.permute(name, array, "seq", perm)

    def to_cross(name, array, step):
        perm = [(s, (s // 2 + step) % chips * 2 + 1 - s % 2) for s in range(groups)]
        return seen.permute(name, array, "seq", perm)

    def to_sibling(name, array):
        return seen.permute(name, array, "seq", [(s, s ^ 1) for s in range(groups)])

    own, other, *rest = cut(queries[0], hit_keys[0], hit_values[0])
    seen.add("cut", own)
    master = seen.after("half", master_weight[0])
    rounded = seen.add("half", half(master, first_moment[0], second_moment[0], gradient[0]))
    pairs = [own, to_sibling("sibling", other)]
    for step in range(1, chips):
        same, cross = rest[4 * step - 4 : 4 * step - 4 + 2]
        pairs += [
            to_same(f"pairs{step}_same", same, step),
            to_cross(f"pairs{step}_cross", cross, step),
        ]
    steps, weights = gather_weights(seen, rounded)
    asked = [()]
    for step in range(1, chips):
        for_same, for_cross = rest[4 * step - 2 : 4 * step]
        asked.append(
            (
                to_same(f"queries{step}_same", for_same, step),
                to_cross(f"queries{step}_cross", for_cross, step),
            )
        )
    own = seen.after("attend0", own)
    attended = [seen.add("attend0", attend(hit_counts, [own] + pairs[1:]))]
    for e, (here, far) in enumerate(asked[1:], 1):
        here = seen.after(f"attend{e}", here)
        attended.append(seen.add(f"attend{e}", attend(hit_counts, pairs, (here, far))))
    spread = [attended] + [
        [to_same(f"attended{e}_to{step}", a, step) for e, a in enumerate(attended)]
        for step in range(1, chips)
    ]
    columns = [None] * groups
    for e in list(range(1, chips)) + [0]:
        att = []
        for d in range(chips):
            a = spread[d][(e - d) % chips]
            att += [a, to_sibling(f"sibling{d}_for{e}", a)]
        att[0] = seen.after(f"project{e}", att[0])
        out, other = project(owner_bucket, att, steps, weights)
        seen.add(f"project{e}", out)
        if e == 0:
            columns[0], columns[1] = out, to_sibling("out_sibling", other)
        else:
            columns[2 * e] = to_same(f"out{e}_same", out, chips - e)
            columns[2 * e + 1] = to_cross(f"out{e}_cross", other, chips - e)
    projected = place(columns)[None]
    states = adam_update(seen.after("states", master_weight), first_moment, second_moment, gradient)
    return (projected, *states)


def solution(mesh):
    return jax.shard_map(
        body,
        mesh=mesh,
        in_specs=(
            P("dp", "seq", None),
            P("dp", "seq", None),
            P("dp", "seq", None),
            P("dp"),
            P("dp", None, "seq"),
            P("dp", None, "seq"),
            P("dp", None, "seq"),
            P("dp", None, "seq"),
            P(),
        ),
        out_specs=(
            P("dp", "seq", None),
            P("dp", None, "seq"),
            P("dp", None, "seq"),
            P("dp", None, "seq"),
        ),
        check_vma=False,
    )
```

```python
import functools
import math

import jax
import jax.numpy as jnp
from jax import lax
from jax.experimental import pallas as pl
from jax.experimental.pallas import tpu as pltpu
from jax.sharding import PartitionSpec as P

HEAD_DIM = 128

beta_one = 0.9
beta_two = 0.999
learn_rate = 0.003
weight_decay = 0.1
epsilon = 1e-08
step_count = 10.0


def adam_update(master_weight, first_moment, second_moment, gradient):
    new_first = beta_one * first_moment + (1.0 - beta_one) * gradient
    new_second = beta_two * second_moment + (1.0 - beta_two) * gradient * gradient
    first_hat = new_first / (1.0 - beta_one**step_count)
    second_hat = new_second / (1.0 - beta_two**step_count)
    new_master = master_weight - learn_rate * (
        first_hat / (jnp.sqrt(second_hat) + epsilon) + weight_decay * master_weight
    )
    return (new_master, new_first, new_second)


ATTEND_US = 3
HALF_STEPS = 2
PROJECT_US = 2

FIRST = {
    "half": ["cut"],
    "queries1_same": ["pairs1_same"],
    "queries1_cross": ["pairs1_same", "pairs1_cross"],
    "attend0": ["swap_own", "back1"],
    "attend1": ["attend0", "back1", "swap_ahead1"],
    "attended1_to1": ["swap_ahead1"],
    "sibling0_for1": ["attended0_to1"],
    "sibling1_for1": ["swap_back1"],
    "sibling0_for0": ["attended0_to1"],
    "project0": ["project1"],
    "states": ["attended0_to1"],
    "sibling": ["half"],
}

SMALL = pltpu.CompilerParams(vmem_limit_bytes=16 * 1024 * 1024)
IN_VMEM = pl.BlockSpec(memory_space=pltpu.VMEM)
IN_SMEM = pl.BlockSpec(memory_space=pltpu.SMEM)


def estimate(micros):
    return pl.CostEstimate(flops=0, bytes_accessed=int(micros * 3.69e6), transcendentals=0)


def chip_and_core():
    me = lax.axis_index("seq")
    return lax.shift_right_logical(me, 1), lax.bitwise_and(me, 1)


def turned(position, step, size):
    moved = position + step
    return jnp.where(moved >= size, moved - size, moved)


class Seen:
    def __init__(self):
        self.values = {}

    def add(self, name, value):
        self.values[name] = value
        return value

    def after(self, name, value):
        others = [self.values[n] for n in FIRST.get(name, ()) if n in self.values]
        return lax.optimization_barrier((value, *others))[0] if others else value

    def permute(self, name, array, axis, perm):
        array = self.after(name, array)
        with jax.named_scope(name):
            return self.add(name, lax.ppermute(array, axis, perm))


def half_kernel(master_ref, first_ref, second_ref, gradient_ref, half_ref):
    new_master, _, _ = adam_update(
        master_ref[...], first_ref[...], second_ref[...], gradient_ref[...]
    )
    half_ref[...] = new_master.astype(jnp.bfloat16)


def half(master_weight, first_moment, second_moment, gradient):
    return pl.pallas_call(
        half_kernel,
        out_shape=jax.ShapeDtypeStruct(master_weight.shape, jnp.bfloat16),
        in_specs=[IN_VMEM] * 4,
        out_specs=IN_VMEM,
        compiler_params=SMALL,
        cost_estimate=estimate(1),
        name="half",
    )(master_weight, first_moment, second_moment, gradient)


def cut_kernel(query, key, value, extra, *refs):
    blocks, brought, sems = refs[:-2], refs[-2], refs[-1]
    chips = (len(blocks) - 2) // 4 + 1
    wide = blocks[0].shape[-1]
    chip, core = chip_and_core()
    copies = []

    def copy(array, step, crossed, target):
        group = 2 * turned(chip, step, chips) + (1 - core if crossed else core)
        lanes = pl.ds(pl.multiple_of(group * wide, wide), wide)
        copies.append(pltpu.make_async_copy(array.at[:, lanes], target, sems.at[len(copies)]))

    for step in range(1, chips):
        for crossed in range(2):
            for i, array in enumerate((key, value)):
                copy(array, step, crossed, blocks[4 * step - 2 + crossed].at[i])
    for crossed in (1, 0):
        for i, array in enumerate((query, key, value)):
            copy(array, 0, crossed, blocks[crossed].at[i])
    for step in range(1, chips):
        for crossed in range(2):
            copy(query, step, crossed, blocks[4 * step + crossed].at[0])
    copies.append(pltpu.make_async_copy(extra, brought, sems.at[len(copies)]))
    for one in copies:
        one.start()
    for one in copies:
        one.wait()


def cut(*arrays):
    groups = lax.axis_size("seq")
    rows, width = arrays[0].shape
    counts = [3, 3] + [2, 2, 1, 1] * (groups // 2 - 1)
    return pl.pallas_call(
        cut_kernel,
        out_shape=[
            jax.ShapeDtypeStruct((n, rows, width // groups), jnp.bfloat16) for n in counts
        ]
        + [jax.ShapeDtypeStruct(arrays[3].shape, arrays[3].dtype)],
        in_specs=[pl.BlockSpec(memory_space=pl.ANY)] * 4,
        out_specs=[IN_VMEM] * (len(counts) + 1),
        scratch_shapes=[pltpu.SemaphoreType.DMA((3 * groups + 1,))],
        compiler_params=SMALL,
        cost_estimate=estimate(1),
        name="cut",
    )(*[pltpu.with_memory_space_constraint(array, pltpu.HBM) for array in arrays])


def attend_kernel(n_pairs, picks, count_ref, *refs):
    pair_refs = refs[:n_pairs]
    out_ref, keys, values = refs[-3:]
    _, rows, wide = out_ref.shape
    chips = n_pairs // 2
    chip, core = chip_and_core()
    columns = []
    for i, ref in enumerate(pair_refs):
        keys[i * rows : (i + 1) * rows, :] = ref[ref.shape[0] - 2]
        values[i * rows : (i + 1) * rows, :] = ref[ref.shape[0] - 1]
        source = 2 * turned(chip, (chips - i // 2) % chips, chips) + (core if i % 2 == 0 else 1 - core)
        columns.append(source * rows + lax.broadcasted_iota(jnp.int32, (1, rows), 1))
    valid = jnp.concatenate(columns, axis=1) < count_ref[0]
    factor = HEAD_DIM ** (-0.5) * math.log2(math.e)
    for block, (at, index) in enumerate(picks):
        for head in range(wide // HEAD_DIM):
            lanes = slice(head * HEAD_DIM, (head + 1) * HEAD_DIM)
            scores = lax.dot_general(
                refs[at][index, :, lanes],
                keys[:, lanes],
                (((1,), (1,)), ((), ())),
                preferred_element_type=jnp.float32,
            )
            scores = jnp.where(valid, scores, -1e30)
            top = jnp.max(scores, axis=1, keepdims=True)
            expo = jnp.exp2((scores - top) * factor)
            total = jnp.sum(expo, axis=1, keepdims=True)
            mixed = jnp.dot(
                expo.astype(jnp.bfloat16), values[:, lanes], preferred_element_type=jnp.float32
            )
            out_ref[block, :, lanes] = (mixed * (1.0 / total)).astype(jnp.bfloat16)


def attend(counts, pairs, queries=()):
    _, rows, wide = pairs[0].shape
    n_pairs = len(pairs)
    picks = ((n_pairs, 0), (n_pairs + 1, 0)) if queries else ((0, 0), (1, 0))
    return pl.pallas_call(
        functools.partial(attend_kernel, n_pairs, picks),
        out_shape=jax.ShapeDtypeStruct((2, rows, wide), jnp.bfloat16),
        in_specs=[IN_SMEM] + [IN_VMEM] * (n_pairs + len(queries)),
        out_specs=IN_VMEM,
        scratch_shapes=[pltpu.VMEM((n_pairs * rows, wide), jnp.bfloat16)] * 2,
        compiler_params=SMALL,
        cost_estimate=estimate(ATTEND_US),
        name="attend",
    )(counts, *pairs, *queries)


def project_kernel(n_att, steps, bucket_ref, *refs):
    att_refs, weight_refs = refs[:n_att], refs[n_att : n_att + 2 * len(steps)]
    out_ref, other_ref, held = refs[n_att + 2 * len(steps) :]
    _, rows, wide = att_refs[0].shape
    depth = weight_refs[0].shape[0]
    parts = wide // depth
    chip, core = chip_and_core()
    owner = lax.axis_index("dp")
    ring = lax.axis_size("dp") // 2
    spot, side = lax.shift_right_logical(owner, 1), lax.bitwise_and(owner, 1)
    for slot, ref in enumerate(att_refs):
        for block in range(2):
            for part in range(parts):
                held[slot * parts + part, block * rows : (block + 1) * rows, :] = ref[
                    block ^ (slot % 2), :, part * depth : (part + 1) * depth
                ]
    total = None
    for i, ref in enumerate(weight_refs):
        from_owner = 2 * turned(spot, steps[i // 2], ring) + (side if i % 2 == 0 else 1 - side)
        bucket = bucket_ref[from_owner]
        group, part = lax.div(bucket, parts), lax.rem(bucket, parts)
        group_chip, group_core = lax.shift_right_logical(group, 1), lax.bitwise_and(group, 1)
        back = chip - group_chip
        back = jnp.where(back < 0, back + n_att // 2, back)
        slot = 2 * back + lax.bitwise_xor(group_core, core)
        term = jnp.dot(held[slot * parts + part], ref[...], preferred_element_type=jnp.float32)
        total = term if total is None else total + term
    total = total.astype(jnp.bfloat16)
    out_ref[...] = total[:rows]
    other_ref[...] = total[rows:]


def project(owner_bucket, att, steps, weights):
    _, rows, wide = att[0].shape
    depth, columns = weights[0].shape
    return pl.pallas_call(
        functools.partial(project_kernel, len(att), steps),
        out_shape=[jax.ShapeDtypeStruct((rows, columns), jnp.bfloat16)] * 2,
        in_specs=[IN_SMEM] + [IN_VMEM] * (len(att) + len(weights)),
        out_specs=[IN_VMEM] * 2,
        scratch_shapes=[pltpu.VMEM((len(att) * wide // depth, 2 * rows, depth), jnp.bfloat16)],
        compiler_params=SMALL,
        cost_estimate=estimate(PROJECT_US),
        name="project",
    )(owner_bucket, *att, *weights)


def place_kernel(n, *refs):
    out_ref = refs[n]
    columns = refs[0].shape[1]
    chip, core = chip_and_core()
    for i in range(n):
        group = 2 * turned(chip, i // 2, n // 2) + (core if i % 2 == 0 else 1 - core)
        out_ref[:, pl.ds(pl.multiple_of(group * columns, columns), columns)] = refs[i][...]


def place(blocks):
    rows, columns = blocks[0].shape
    return pl.pallas_call(
        functools.partial(place_kernel, len(blocks)),
        out_shape=jax.ShapeDtypeStruct((rows, columns * len(blocks)), jnp.bfloat16),
        in_specs=[IN_VMEM] * len(blocks),
        out_specs=IN_VMEM,
        compiler_params=SMALL,
        cost_estimate=estimate(1),
        name="place",
    )(*blocks)


def gather_weights(seen, shard):
    owners = lax.axis_size("dp")
    ring = owners // 2

    def moved(block, step, name):
        perm = [(o, (o // 2 + step) % ring * 2 + o % 2) for o in range(owners)]
        return seen.permute(name, block, "dp", perm)

    held = [(0, shard, "swap_own")]
    ahead = back = shard
    for step in range(1, ring // 2 + 1):
        ahead = moved(ahead, 1, f"ahead{step}")
        held.append((-step % ring, ahead, f"swap_ahead{step}"))
        if step <= (ring - 1) // 2:
            back = moved(back, -1, f"back{step}")
            held.append((step, back, f"swap_back{step}"))
    blocks = []
    for _, block, name in held:
        swapped = seen.permute(name, block, "dp", [(o, o ^ 1) for o in range(owners)])
        blocks += [block, swapped]
    return [step for step, _, _ in held], blocks


def body(
    queries,
    hit_keys,
    hit_values,
    hit_counts,
    master_weight,
    first_moment,
    second_moment,
    gradient,
    owner_bucket,
):
    groups = lax.axis_size("seq")
    chips = groups // 2
    seen = Seen()

    def to_same(name, array, step):
        perm = [(s, (s // 2 + step) % chips * 2 + s % 2) for s in range(groups)]
        return seen.permute(name, array, "seq", perm)

    def to_cross(name, array, step):
        perm = [(s, (s // 2 + step) % chips * 2 + 1 - s % 2) for s in range(groups)]
        return seen.permute(name, array, "seq", perm)

    def to_sibling(name, array):
        return seen.permute(name, array, "seq", [(s, s ^ 1) for s in range(groups)])

    own, other, *rest, grad = cut(queries[0], hit_keys[0], hit_values[0], gradient[0])
    seen.add("cut", own)
    master = seen.after("half", master_weight[0])
    rounded = seen.add("half", half(master, first_moment[0], second_moment[0], grad))
    pairs = []
    for step in range(1, chips):
        same, cross = rest[4 * step - 4 : 4 * step - 4 + 2]
        pairs += [
            to_same(f"pairs{step}_same", same, step),
            to_cross(f"pairs{step}_cross", cross, step),
        ]
    steps, weights = gather_weights(seen, rounded)
    pairs = [own, to_sibling("sibling", other)] + pairs
    asked = [()]
    for step in range(1, chips):
        for_same, for_cross = rest[4 * step - 2 : 4 * step]
        asked.append(
            (
                to_same(f"queries{step}_same", for_same, step),
                to_cross(f"queries{step}_cross", for_cross, step),
            )
        )
    own = seen.after("attend0", own)
    attended = [seen.add("attend0", attend(hit_counts, [own] + pairs[1:]))]
    for e, (here, far) in enumerate(asked[1:], 1):
        here = seen.after(f"attend{e}", here)
        attended.append(seen.add(f"attend{e}", attend(hit_counts, pairs, (here, far))))
    spread = [attended] + [
        [to_same(f"attended{e}_to{step}", a, step) for e, a in enumerate(attended)]
        for step in range(1, chips)
    ]
    columns = [None] * groups
    for e in list(range(1, chips)) + [0]:
        att = []
        for d in range(chips):
            a = spread[d][(e - d) % chips]
            att += [a, to_sibling(f"sibling{d}_for{e}", a)]
        att[0] = seen.after(f"project{e}", att[0])
        out, other = project(owner_bucket, att, steps, weights)
        seen.add(f"project{e}", out)
        if e == 0:
            columns[0], columns[1] = out, to_sibling("out_sibling", other)
        else:
            columns[2 * e] = to_same(f"out{e}_same", out, chips - e)
            columns[2 * e + 1] = to_cross(f"out{e}_cross", other, chips - e)
    projected = place(columns)[None]
    states = adam_update(seen.after("states", master_weight), first_moment, second_moment, gradient)
    return (projected, *states)


def solution(mesh):
    return jax.shard_map(
        body,
        mesh=mesh,
        in_specs=(
            P("dp", "seq", None),
            P("dp", "seq", None),
            P("dp", "seq", None),
            P("dp"),
            P("dp", None, "seq"),
            P("dp", None, "seq"),
            P("dp", None, "seq"),
            P("dp", None, "seq"),
            P(),
        ),
        out_specs=(
            P("dp", "seq", None),
            P("dp", None, "seq"),
            P("dp", None, "seq"),
            P("dp", None, "seq"),
        ),
        check_vma=False,
    )
```

```python
import functools
import math

import jax
import jax.numpy as jnp
from jax import lax
from jax.experimental import pallas as pl
from jax.experimental.pallas import tpu as pltpu
from jax.sharding import PartitionSpec as P

HEAD_DIM = 128

beta_one = 0.9
beta_two = 0.999
learn_rate = 0.003
weight_decay = 0.1
epsilon = 1e-08
step_count = 10.0


def adam_update(master_weight, first_moment, second_moment, gradient):
    new_first = beta_one * first_moment + (1.0 - beta_one) * gradient
    new_second = beta_two * second_moment + (1.0 - beta_two) * gradient * gradient
    first_hat = new_first / (1.0 - beta_one**step_count)
    second_hat = new_second / (1.0 - beta_two**step_count)
    new_master = master_weight - learn_rate * (
        first_hat / (jnp.sqrt(second_hat) + epsilon) + weight_decay * master_weight
    )
    return (new_master, new_first, new_second)


ATTEND_US = 3
HALF_STEPS = 2
PROJECT_US = 2

FIRST = {
    "half": ["cut"],
    "queries1_same": ["pairs1_same"],
    "queries1_cross": ["pairs1_same", "pairs1_cross"],
    "attend0": ["swap_own", "back1"],
    "attend1": ["attend0", "back1", "swap_ahead1"],
    "attended1_to1": ["swap_ahead1"],
    "sibling0_for1": ["attended0_to1"],
    "sibling1_for1": ["swap_back1"],
    "sibling0_for0": ["attended0_to1"],
    "project0": ["project1"],
    "states": ["attended0_to1"],
    "sibling": ["half"],
}

SMALL = pltpu.CompilerParams(vmem_limit_bytes=16 * 1024 * 1024)
IN_VMEM = pl.BlockSpec(memory_space=pltpu.VMEM)
IN_SMEM = pl.BlockSpec(memory_space=pltpu.SMEM)


def estimate(micros):
    return pl.CostEstimate(flops=0, bytes_accessed=int(micros * 3.69e6), transcendentals=0)


def chip_and_core():
    me = lax.axis_index("seq")
    return lax.shift_right_logical(me, 1), lax.bitwise_and(me, 1)


def turned(position, step, size):
    moved = position + step
    return jnp.where(moved >= size, moved - size, moved)


class Seen:
    def __init__(self):
        self.values = {}

    def add(self, name, value):
        self.values[name] = value
        return value

    def after(self, name, value):
        others = [self.values[n] for n in FIRST.get(name, ()) if n in self.values]
        return lax.optimization_barrier((value, *others))[0] if others else value

    def permute(self, name, array, axis, perm):
        array = self.after(name, array)
        with jax.named_scope(name):
            return self.add(name, lax.ppermute(array, axis, perm))


def half_kernel(master_ref, first_ref, second_ref, gradient_ref, half_ref):
    new_master, _, _ = adam_update(
        master_ref[...], first_ref[...], second_ref[...], gradient_ref[...]
    )
    half_ref[...] = new_master.astype(jnp.bfloat16)


def half(master_weight, first_moment, second_moment, gradient):
    return pl.pallas_call(
        half_kernel,
        out_shape=jax.ShapeDtypeStruct(master_weight.shape, jnp.bfloat16),
        in_specs=[IN_VMEM] * 4,
        out_specs=IN_VMEM,
        compiler_params=SMALL,
        cost_estimate=estimate(1),
        name="half",
    )(master_weight, first_moment, second_moment, gradient)


def cut_kernel(query, key, value, extra, *refs):
    blocks, brought, sems = refs[:-2], refs[-2], refs[-1]
    chips = (len(blocks) - 2) // 4 + 1
    wide = blocks[0].shape[-1]
    chip, core = chip_and_core()
    copies = []

    def copy(array, step, crossed, target):
        group = 2 * turned(chip, step, chips) + (1 - core if crossed else core)
        lanes = pl.ds(pl.multiple_of(group * wide, wide), wide)
        copies.append(pltpu.make_async_copy(array.at[:, lanes], target, sems.at[len(copies)]))

    for step in range(1, chips):
        for crossed in range(2):
            for i, array in enumerate((key, value)):
                copy(array, step, crossed, blocks[4 * step - 2 + crossed].at[i])
    for crossed in (1, 0):
        for i, array in enumerate((query, key, value)):
            copy(array, 0, crossed, blocks[crossed].at[i])
    for step in range(1, chips):
        for crossed in range(2):
            copy(query, step, crossed, blocks[4 * step + crossed].at[0])
    copies.append(pltpu.make_async_copy(extra, brought, sems.at[len(copies)]))
    for one in copies:
        one.start()
    for one in copies:
        one.wait()


def cut(*arrays):
    groups = lax.axis_size("seq")
    rows, width = arrays[0].shape
    counts = [3, 3] + [2, 2, 1, 1] * (groups // 2 - 1)
    return pl.pallas_call(
        cut_kernel,
        out_shape=[
            jax.ShapeDtypeStruct((n, rows, width // groups), jnp.bfloat16) for n in counts
        ]
        + [jax.ShapeDtypeStruct(arrays[3].shape, arrays[3].dtype)],
        in_specs=[pl.BlockSpec(memory_space=pl.ANY)] * 4,
        out_specs=[IN_VMEM] * (len(counts) + 1),
        scratch_shapes=[pltpu.SemaphoreType.DMA((3 * groups + 1,))],
        compiler_params=SMALL,
        cost_estimate=estimate(1),
        name="cut",
    )(*[pltpu.with_memory_space_constraint(array, pltpu.HBM) for array in arrays])


def attend_kernel(n_pairs, picks, count_ref, *refs):
    pair_refs = refs[:n_pairs]
    out_ref, keys, values = refs[-3:]
    _, rows, wide = out_ref.shape
    chips = n_pairs // 2
    chip, core = chip_and_core()
    columns = []
    for i, ref in enumerate(pair_refs):
        keys[i * rows : (i + 1) * rows, :] = ref[ref.shape[0] - 2]
        values[i * rows : (i + 1) * rows, :] = ref[ref.shape[0] - 1]
        source = 2 * turned(chip, (chips - i // 2) % chips, chips) + (core if i % 2 == 0 else 1 - core)
        columns.append(source * rows + lax.broadcasted_iota(jnp.int32, (1, rows), 1))
    valid = jnp.concatenate(columns, axis=1) < count_ref[0]
    factor = HEAD_DIM ** (-0.5) * math.log2(math.e)
    for block, (at, index) in enumerate(picks):
        for head in range(wide // HEAD_DIM):
            lanes = slice(head * HEAD_DIM, (head + 1) * HEAD_DIM)
            scores = lax.dot_general(
                refs[at][index, :, lanes],
                keys[:, lanes],
                (((1,), (1,)), ((), ())),
                preferred_element_type=jnp.float32,
            )
            scores = jnp.where(valid, scores, -1e30)
            top = jnp.max(scores, axis=1, keepdims=True)
            expo = jnp.exp2((scores - top) * factor)
            total = jnp.sum(expo, axis=1, keepdims=True)
            mixed = jnp.dot(
                expo.astype(jnp.bfloat16), values[:, lanes], preferred_element_type=jnp.float32
            )
            out_ref[block, :, lanes] = (mixed * (1.0 / total)).astype(jnp.bfloat16)


def attend(counts, pairs, queries=()):
    _, rows, wide = pairs[0].shape
    n_pairs = len(pairs)
    picks = ((n_pairs, 0), (n_pairs + 1, 0)) if queries else ((0, 0), (1, 0))
    return pl.pallas_call(
        functools.partial(attend_kernel, n_pairs, picks),
        out_shape=jax.ShapeDtypeStruct((2, rows, wide), jnp.bfloat16),
        in_specs=[IN_SMEM] + [IN_VMEM] * (n_pairs + len(queries)),
        out_specs=IN_VMEM,
        scratch_shapes=[pltpu.VMEM((n_pairs * rows, wide), jnp.bfloat16)] * 2,
        compiler_params=SMALL,
        cost_estimate=estimate(ATTEND_US),
        name="attend",
    )(counts, *pairs, *queries)


def project_kernel(n_att, steps, bucket_ref, *refs):
    att_refs, weight_refs = refs[:n_att], refs[n_att : n_att + 2 * len(steps)]
    out_ref, other_ref, held = refs[n_att + 2 * len(steps) :]
    _, rows, wide = att_refs[0].shape
    depth = weight_refs[0].shape[0]
    parts = wide // depth
    chip, core = chip_and_core()
    owner = lax.axis_index("dp")
    ring = lax.axis_size("dp") // 2
    spot, side = lax.shift_right_logical(owner, 1), lax.bitwise_and(owner, 1)
    for slot, ref in enumerate(att_refs):
        for block in range(2):
            for part in range(parts):
                held[slot * parts + part, block * rows : (block + 1) * rows, :] = ref[
                    block ^ (slot % 2), :, part * depth : (part + 1) * depth
                ]
    total = None
    for i, ref in enumerate(weight_refs):
        from_owner = 2 * turned(spot, steps[i // 2], ring) + (side if i % 2 == 0 else 1 - side)
        bucket = bucket_ref[from_owner]
        group, part = lax.div(bucket, parts), lax.rem(bucket, parts)
        group_chip, group_core = lax.shift_right_logical(group, 1), lax.bitwise_and(group, 1)
        back = chip - group_chip
        back = jnp.where(back < 0, back + n_att // 2, back)
        slot = 2 * back + lax.bitwise_xor(group_core, core)
        term = jnp.dot(held[slot * parts + part], ref[...], preferred_element_type=jnp.float32)
        total = term if total is None else total + term
    total = total.astype(jnp.bfloat16)
    out_ref[...] = total[:rows]
    other_ref[...] = total[rows:]


def project(owner_bucket, att, steps, weights):
    _, rows, wide = att[0].shape
    depth, columns = weights[0].shape
    return pl.pallas_call(
        functools.partial(project_kernel, len(att), steps),
        out_shape=[jax.ShapeDtypeStruct((rows, columns), jnp.bfloat16)] * 2,
        in_specs=[IN_SMEM] + [IN_VMEM] * (len(att) + len(weights)),
        out_specs=[IN_VMEM] * 2,
        scratch_shapes=[pltpu.VMEM((len(att) * wide // depth, 2 * rows, depth), jnp.bfloat16)],
        compiler_params=SMALL,
        cost_estimate=estimate(PROJECT_US),
        name="project",
    )(owner_bucket, *att, *weights)


def place_kernel(n, *refs):
    out_ref, sems = refs[n:]
    columns = refs[0].shape[1]
    chip, core = chip_and_core()
    copies = []
    for i in range(n):
        group = 2 * turned(chip, i // 2, n // 2) + (core if i % 2 == 0 else 1 - core)
        lanes = pl.ds(pl.multiple_of(group * columns, columns), columns)
        copies.append(pltpu.make_async_copy(refs[i], out_ref.at[:, lanes], sems.at[i]))
        copies[-1].start()
    for copy in copies:
        copy.wait()


def place(blocks):
    rows, columns = blocks[0].shape
    return pl.pallas_call(
        functools.partial(place_kernel, len(blocks)),
        out_shape=jax.ShapeDtypeStruct((rows, columns * len(blocks)), jnp.bfloat16),
        in_specs=[IN_VMEM] * len(blocks),
        out_specs=pl.BlockSpec(memory_space=pltpu.HBM),
        scratch_shapes=[pltpu.SemaphoreType.DMA((len(blocks),))],
        compiler_params=SMALL,
        cost_estimate=estimate(1),
        name="place",
    )(*blocks)


def gather_weights(seen, shard):
    owners = lax.axis_size("dp")
    ring = owners // 2

    def moved(block, step, name):
        perm = [(o, (o // 2 + step) % ring * 2 + o % 2) for o in range(owners)]
        return seen.permute(name, block, "dp", perm)

    held = [(0, shard, "swap_own")]
    ahead = back = shard
    for step in range(1, ring // 2 + 1):
        ahead = moved(ahead, 1, f"ahead{step}")
        held.append((-step % ring, ahead, f"swap_ahead{step}"))
        if step <= (ring - 1) // 2:
            back = moved(back, -1, f"back{step}")
            held.append((step, back, f"swap_back{step}"))
    blocks = []
    for _, block, name in held:
        swapped = seen.permute(name, block, "dp", [(o, o ^ 1) for o in range(owners)])
        blocks += [block, swapped]
    return [step for step, _, _ in held], blocks


def body(
    queries,
    hit_keys,
    hit_values,
    hit_counts,
    master_weight,
    first_moment,
    second_moment,
    gradient,
    owner_bucket,
):
    groups = lax.axis_size("seq")
    chips = groups // 2
    seen = Seen()

    def to_same(name, array, step):
        perm = [(s, (s // 2 + step) % chips * 2 + s % 2) for s in range(groups)]
        return seen.permute(name, array, "seq", perm)

    def to_cross(name, array, step):
        perm = [(s, (s // 2 + step) % chips * 2 + 1 - s % 2) for s in range(groups)]
        return seen.permute(name, array, "seq", perm)

    def to_sibling(name, array):
        return seen.permute(name, array, "seq", [(s, s ^ 1) for s in range(groups)])

    own, other, *rest, grad = cut(queries[0], hit_keys[0], hit_values[0], gradient[0])
    seen.add("cut", own)
    master = seen.after("half", master_weight[0])
    rounded = seen.add("half", half(master, first_moment[0], second_moment[0], grad))
    pairs = []
    for step in range(1, chips):
        same, cross = rest[4 * step - 4 : 4 * step - 4 + 2]
        pairs += [
            to_same(f"pairs{step}_same", same, step),
            to_cross(f"pairs{step}_cross", cross, step),
        ]
    steps, weights = gather_weights(seen, rounded)
    pairs = [own, to_sibling("sibling", other)] + pairs
    asked = [()]
    for step in range(1, chips):
        for_same, for_cross = rest[4 * step - 2 : 4 * step]
        asked.append(
            (
                to_same(f"queries{step}_same", for_same, step),
                to_cross(f"queries{step}_cross", for_cross, step),
            )
        )
    own = seen.after("attend0", own)
    attended = [seen.add("attend0", attend(hit_counts, [own] + pairs[1:]))]
    for e, (here, far) in enumerate(asked[1:], 1):
        here = seen.after(f"attend{e}", here)
        attended.append(seen.add(f"attend{e}", attend(hit_counts, pairs, (here, far))))
    spread = [attended] + [
        [to_same(f"attended{e}_to{step}", a, step) for e, a in enumerate(attended)]
        for step in range(1, chips)
    ]
    columns = [None] * groups
    for e in list(range(1, chips)) + [0]:
        att = []
        for d in range(chips):
            a = spread[d][(e - d) % chips]
            att += [a, to_sibling(f"sibling{d}_for{e}", a)]
        att[0] = seen.after(f"project{e}", att[0])
        out, other = project(owner_bucket, att, steps, weights)
        seen.add(f"project{e}", out)
        if e == 0:
            columns[0], columns[1] = out, to_sibling("out_sibling", other)
        else:
            columns[2 * e] = to_same(f"out{e}_same", out, chips - e)
            columns[2 * e + 1] = to_cross(f"out{e}_cross", other, chips - e)
    projected = place(columns)[None]
    states = adam_update(seen.after("states", master_weight), first_moment, second_moment, gradient)
    return (projected, *states)


def solution(mesh):
    return jax.shard_map(
        body,
        mesh=mesh,
        in_specs=(
            P("dp", "seq", None),
            P("dp", "seq", None),
            P("dp", "seq", None),
            P("dp"),
            P("dp", None, "seq"),
            P("dp", None, "seq"),
            P("dp", None, "seq"),
            P("dp", None, "seq"),
            P(),
        ),
        out_specs=(
            P("dp", "seq", None),
            P("dp", None, "seq"),
            P("dp", None, "seq"),
            P("dp", None, "seq"),
        ),
        check_vma=False,
    )
```

```python
import functools
import math

import jax
import jax.numpy as jnp
from jax import lax
from jax.experimental import pallas as pl
from jax.experimental.pallas import tpu as pltpu
from jax.sharding import PartitionSpec as P

HEAD_DIM = 128

beta_one = 0.9
beta_two = 0.999
learn_rate = 0.003
weight_decay = 0.1
epsilon = 1e-08
step_count = 10.0


def adam_update(master_weight, first_moment, second_moment, gradient):
    new_first = beta_one * first_moment + (1.0 - beta_one) * gradient
    new_second = beta_two * second_moment + (1.0 - beta_two) * gradient * gradient
    first_hat = new_first / (1.0 - beta_one**step_count)
    second_hat = new_second / (1.0 - beta_two**step_count)
    new_master = master_weight - learn_rate * (
        first_hat / (jnp.sqrt(second_hat) + epsilon) + weight_decay * master_weight
    )
    return (new_master, new_first, new_second)


ATTEND_US = 3
HALF_STEPS = 2
PROJECT_US = 2

FIRST = {
    "half": ["cut"],
    "queries1_same": ["pairs1_same"],
    "queries1_cross": ["pairs1_same", "pairs1_cross"],
    "attend0": ["swap_own", "back1"],
    "attend1": ["attend0"],
    "attended1_to1": ["swap_ahead1"],
    "sibling0_for1": ["attended0_to1"],
    "sibling1_for1": ["swap_back1"],
    "sibling0_for0": ["attended0_to1"],
    "project0": ["project1"],
    "states": ["attended0_to1"],
}

SMALL = pltpu.CompilerParams(vmem_limit_bytes=16 * 1024 * 1024)
IN_VMEM = pl.BlockSpec(memory_space=pltpu.VMEM)
IN_SMEM = pl.BlockSpec(memory_space=pltpu.SMEM)


def estimate(micros):
    return pl.CostEstimate(flops=0, bytes_accessed=int(micros * 3.69e6), transcendentals=0)


def chip_and_core():
    me = lax.axis_index("seq")
    return lax.shift_right_logical(me, 1), lax.bitwise_and(me, 1)


def turned(position, step, size):
    moved = position + step
    return jnp.where(moved >= size, moved - size, moved)


class Seen:
    def __init__(self):
        self.values = {}

    def add(self, name, value):
        self.values[name] = value
        return value

    def after(self, name, value):
        others = [self.values[n] for n in FIRST.get(name, ()) if n in self.values]
        return lax.optimization_barrier((value, *others))[0] if others else value

    def permute(self, name, array, axis, perm):
        array = self.after(name, array)
        with jax.named_scope(name):
            return self.add(name, lax.ppermute(array, axis, perm))


def half_kernel(master_ref, first_ref, second_ref, gradient_ref, half_ref):
    new_master, _, _ = adam_update(
        master_ref[...], first_ref[...], second_ref[...], gradient_ref[...]
    )
    half_ref[...] = new_master.astype(jnp.bfloat16)


def half(master_weight, first_moment, second_moment, gradient):
    return pl.pallas_call(
        half_kernel,
        out_shape=jax.ShapeDtypeStruct(master_weight.shape, jnp.bfloat16),
        in_specs=[IN_VMEM] * 4,
        out_specs=IN_VMEM,
        compiler_params=SMALL,
        cost_estimate=estimate(1),
        name="half",
    )(master_weight, first_moment, second_moment, gradient)


def cut_kernel(query, key, value, extra, *refs):
    blocks, brought, sems = refs[:-2], refs[-2], refs[-1]
    chips = (len(blocks) - 2) // 4 + 1
    wide = blocks[0].shape[-1]
    chip, core = chip_and_core()
    copies = []

    def copy(array, step, crossed, target):
        group = 2 * turned(chip, step, chips) + (1 - core if crossed else core)
        lanes = pl.ds(pl.multiple_of(group * wide, wide), wide)
        copies.append(pltpu.make_async_copy(array.at[:, lanes], target, sems.at[len(copies)]))

    for step in range(1, chips):
        for crossed in range(2):
            for i, array in enumerate((key, value)):
                copy(array, step, crossed, blocks[4 * step - 2 + crossed].at[i])
    for crossed in (1, 0):
        for i, array in enumerate((query, key, value)):
            copy(array, 0, crossed, blocks[crossed].at[i])
    for step in range(1, chips):
        for crossed in range(2):
            copy(query, step, crossed, blocks[4 * step + crossed].at[0])
    copies.append(pltpu.make_async_copy(extra, brought, sems.at[len(copies)]))
    for one in copies:
        one.start()
    for one in copies:
        one.wait()


def cut(*arrays):
    groups = lax.axis_size("seq")
    rows, width = arrays[0].shape
    counts = [3, 3] + [2, 2, 1, 1] * (groups // 2 - 1)
    return pl.pallas_call(
        cut_kernel,
        out_shape=[
            jax.ShapeDtypeStruct((n, rows, width // groups), jnp.bfloat16) for n in counts
        ]
        + [jax.ShapeDtypeStruct(arrays[3].shape, arrays[3].dtype)],
        in_specs=[pl.BlockSpec(memory_space=pl.ANY)] * 4,
        out_specs=[IN_VMEM] * (len(counts) + 1),
        scratch_shapes=[pltpu.SemaphoreType.DMA((3 * groups + 1,))],
        compiler_params=SMALL,
        cost_estimate=estimate(1),
        name="cut",
    )(*[pltpu.with_memory_space_constraint(array, pltpu.HBM) for array in arrays])


def attend_kernel(n_pairs, picks, count_ref, *refs):
    pair_refs = refs[:n_pairs]
    out_ref, keys, values = refs[-3:]
    _, rows, wide = out_ref.shape
    chips = n_pairs // 2
    chip, core = chip_and_core()
    columns = []
    for i, ref in enumerate(pair_refs):
        keys[i * rows : (i + 1) * rows, :] = ref[ref.shape[0] - 2]
        values[i * rows : (i + 1) * rows, :] = ref[ref.shape[0] - 1]
        source = 2 * turned(chip, (chips - i // 2) % chips, chips) + (core if i % 2 == 0 else 1 - core)
        columns.append(source * rows + lax.broadcasted_iota(jnp.int32, (1, rows), 1))
    valid = jnp.concatenate(columns, axis=1) < count_ref[0]
    factor = HEAD_DIM ** (-0.5) * math.log2(math.e)
    for block, (at, index) in enumerate(picks):
        for head in range(wide // HEAD_DIM):
            lanes = slice(head * HEAD_DIM, (head + 1) * HEAD_DIM)
            scores = lax.dot_general(
                refs[at][index, :, lanes],
                keys[:, lanes],
                (((1,), (1,)), ((), ())),
                preferred_element_type=jnp.float32,
            )
            scores = jnp.where(valid, scores, -1e30)
            top = jnp.max(scores, axis=1, keepdims=True)
            expo = jnp.exp2((scores - top) * factor)
            total = jnp.sum(expo, axis=1, keepdims=True)
            mixed = jnp.dot(
                expo.astype(jnp.bfloat16), values[:, lanes], preferred_element_type=jnp.float32
            )
            out_ref[block, :, lanes] = (mixed * (1.0 / total)).astype(jnp.bfloat16)


def attend(counts, pairs, queries=()):
    _, rows, wide = pairs[0].shape
    n_pairs = len(pairs)
    picks = ((n_pairs, 0), (n_pairs + 1, 0)) if queries else ((0, 0), (1, 0))
    return pl.pallas_call(
        functools.partial(attend_kernel, n_pairs, picks),
        out_shape=jax.ShapeDtypeStruct((2, rows, wide), jnp.bfloat16),
        in_specs=[IN_SMEM] + [IN_VMEM] * (n_pairs + len(queries)),
        out_specs=IN_VMEM,
        scratch_shapes=[pltpu.VMEM((n_pairs * rows, wide), jnp.bfloat16)] * 2,
        compiler_params=SMALL,
        cost_estimate=estimate(ATTEND_US),
        name="attend",
    )(counts, *pairs, *queries)


def project_kernel(n_att, steps, bucket_ref, *refs):
    att_refs, weight_refs = refs[:n_att], refs[n_att : n_att + 2 * len(steps)]
    out_ref, other_ref, held = refs[n_att + 2 * len(steps) :]
    _, rows, wide = att_refs[0].shape
    depth = weight_refs[0].shape[0]
    parts = wide // depth
    chip, core = chip_and_core()
    owner = lax.axis_index("dp")
    ring = lax.axis_size("dp") // 2
    spot, side = lax.shift_right_logical(owner, 1), lax.bitwise_and(owner, 1)
    for slot, ref in enumerate(att_refs):
        for block in range(2):
            for part in range(parts):
                held[slot * parts + part, block * rows : (block + 1) * rows, :] = ref[
                    block ^ (slot % 2), :, part * depth : (part + 1) * depth
                ]
    total = None
    for i, ref in enumerate(weight_refs):
        from_owner = 2 * turned(spot, steps[i // 2], ring) + (side if i % 2 == 0 else 1 - side)
        bucket = bucket_ref[from_owner]
        group, part = lax.div(bucket, parts), lax.rem(bucket, parts)
        group_chip, group_core = lax.shift_right_logical(group, 1), lax.bitwise_and(group, 1)
        back = chip - group_chip
        back = jnp.where(back < 0, back + n_att // 2, back)
        slot = 2 * back + lax.bitwise_xor(group_core, core)
        term = jnp.dot(held[slot * parts + part], ref[...], preferred_element_type=jnp.float32)
        total = term if total is None else total + term
    total = total.astype(jnp.bfloat16)
    out_ref[...] = total[:rows]
    other_ref[...] = total[rows:]


def project(owner_bucket, att, steps, weights):
    _, rows, wide = att[0].shape
    depth, columns = weights[0].shape
    return pl.pallas_call(
        functools.partial(project_kernel, len(att), steps),
        out_shape=[jax.ShapeDtypeStruct((rows, columns), jnp.bfloat16)] * 2,
        in_specs=[IN_SMEM] + [IN_VMEM] * (len(att) + len(weights)),
        out_specs=[IN_VMEM] * 2,
        scratch_shapes=[pltpu.VMEM((len(att) * wide // depth, 2 * rows, depth), jnp.bfloat16)],
        compiler_params=SMALL,
        cost_estimate=estimate(PROJECT_US),
        name="project",
    )(owner_bucket, *att, *weights)


def place_kernel(n, *refs):
    out_ref = refs[n]
    columns = refs[0].shape[1]
    chip, core = chip_and_core()
    for i in range(n):
        group = 2 * turned(chip, i // 2, n // 2) + (core if i % 2 == 0 else 1 - core)
        out_ref[:, pl.ds(pl.multiple_of(group * columns, columns), columns)] = refs[i][...]


def place(blocks):
    rows, columns = blocks[0].shape
    return pl.pallas_call(
        functools.partial(place_kernel, len(blocks)),
        out_shape=jax.ShapeDtypeStruct((rows, columns * len(blocks)), jnp.bfloat16),
        in_specs=[IN_VMEM] * len(blocks),
        out_specs=IN_VMEM,
        compiler_params=SMALL,
        cost_estimate=estimate(1),
        name="place",
    )(*blocks)


def gather_weights(seen, shard):
    owners = lax.axis_size("dp")
    ring = owners // 2

    def moved(block, step, name):
        perm = [(o, (o // 2 + step) % ring * 2 + o % 2) for o in range(owners)]
        return seen.permute(name, block, "dp", perm)

    held = [(0, shard, "swap_own")]
    ahead = back = shard
    for step in range(1, ring // 2 + 1):
        ahead = moved(ahead, 1, f"ahead{step}")
        held.append((-step % ring, ahead, f"swap_ahead{step}"))
        if step <= (ring - 1) // 2:
            back = moved(back, -1, f"back{step}")
            held.append((step, back, f"swap_back{step}"))
    blocks = []
    for _, block, name in held:
        swapped = seen.permute(name, block, "dp", [(o, o ^ 1) for o in range(owners)])
        blocks += [block, swapped]
    return [step for step, _, _ in held], blocks


def body(
    queries,
    hit_keys,
    hit_values,
    hit_counts,
    master_weight,
    first_moment,
    second_moment,
    gradient,
    owner_bucket,
):
    groups = lax.axis_size("seq")
    chips = groups // 2
    seen = Seen()

    def to_same(name, array, step):
        perm = [(s, (s // 2 + step) % chips * 2 + s % 2) for s in range(groups)]
        return seen.permute(name, array, "seq", perm)

    def to_cross(name, array, step):
        perm = [(s, (s // 2 + step) % chips * 2 + 1 - s % 2) for s in range(groups)]
        return seen.permute(name, array, "seq", perm)

    def to_sibling(name, array):
        return seen.permute(name, array, "seq", [(s, s ^ 1) for s in range(groups)])

    own, other, *rest, grad = cut(queries[0], hit_keys[0], hit_values[0], gradient[0])
    seen.add("cut", own)
    master = seen.after("half", master_weight[0])
    rounded = seen.add("half", half(master, first_moment[0], second_moment[0], grad))
    pairs = []
    for step in range(1, chips):
        same, cross = rest[4 * step - 4 : 4 * step - 4 + 2]
        pairs += [
            to_same(f"pairs{step}_same", same, step),
            to_cross(f"pairs{step}_cross", cross, step),
        ]
    steps, weights = gather_weights(seen, rounded)
    pairs = [own, to_sibling("sibling", other)] + pairs
    asked = [()]
    for step in range(1, chips):
        for_same, for_cross = rest[4 * step - 2 : 4 * step]
        asked.append(
            (
                to_same(f"queries{step}_same", for_same, step),
                to_cross(f"queries{step}_cross", for_cross, step),
            )
        )
    own = seen.after("attend0", own)
    attended = [seen.add("attend0", attend(hit_counts, [own] + pairs[1:]))]
    for e, (here, far) in enumerate(asked[1:], 1):
        here = seen.after(f"attend{e}", here)
        attended.append(seen.add(f"attend{e}", attend(hit_counts, pairs, (here, far))))
    spread = [attended] + [
        [to_same(f"attended{e}_to{step}", a, step) for e, a in enumerate(attended)]
        for step in range(1, chips)
    ]
    columns = [None] * groups
    for e in list(range(1, chips)) + [0]:
        att = []
        for d in range(chips):
            a = spread[d][(e - d) % chips]
            att += [a, to_sibling(f"sibling{d}_for{e}", a)]
        att[0] = seen.after(f"project{e}", att[0])
        out, other = project(owner_bucket, att, steps, weights)
        seen.add(f"project{e}", out)
        if e == 0:
            columns[0], columns[1] = out, to_sibling("out_sibling", other)
        else:
            columns[2 * e] = to_same(f"out{e}_same", out, chips - e)
            columns[2 * e + 1] = to_cross(f"out{e}_cross", other, chips - e)
    projected = place(columns)[None]
    states = adam_update(seen.after("states", master_weight), first_moment, second_moment, gradient)
    return (projected, *states)


def solution(mesh):
    return jax.shard_map(
        body,
        mesh=mesh,
        in_specs=(
            P("dp", "seq", None),
            P("dp", "seq", None),
            P("dp", "seq", None),
            P("dp"),
            P("dp", None, "seq"),
            P("dp", None, "seq"),
            P("dp", None, "seq"),
            P("dp", None, "seq"),
            P(),
        ),
        out_specs=(
            P("dp", "seq", None),
            P("dp", None, "seq"),
            P("dp", None, "seq"),
            P("dp", None, "seq"),
        ),
        check_vma=False,
    )
```
